32 devices in a mesh: ctx: 8 (over y, x, core), head: 4 (over z).
Axes of the slice: x: 2, y: 2, z: 4, core: 2. Of those that a mesh axis runs over, the one named last changes fastest.
Arguments:
- inputs: bfloat16 [2048, 4096], P('ctx', 'head'), may hold values from -6 to 6
- log_decay: float32 [64, 2048], P('head', 'ctx'), may hold values from -1 to 0
- in_b: bfloat16 [2048, 512], P('ctx', 'head'), may hold values from -0.20996094 to 0.20996094
- in_c: bfloat16 [2048, 512], P('ctx', 'head'), may hold values from -0.20996094 to 0.20996094
- seg_ids: int32 [2048], P('ctx'), may hold values from 0 to 5, never falling along the last dimension, each value on 1 to 1024 neighbouring positions
- skip_gain: float32 [64], P('head'), may hold values from 0.1 to 1.9
- grad_out: bfloat16 [2048, 4096], P('ctx', 'head'), may hold values from -0.119628906 to 0.119628906
Outputs:
- ssd_out: bfloat16 [2048, 4096], P('ctx', 'head')
- grad_x: bfloat16 [2048, 4096], P('ctx', 'head')
- grad_b: bfloat16 [2048, 512], P('ctx', 'head')
- grad_c: bfloat16 [2048, 512], P('ctx', 'head')
The draws below stay inside these ranges and needn't reach their ends.
All inputs are finite; a program needn't handle non-finite values.
Results may differ from the reference program's by a relative error of at most 0.0017.
Values may be sent and summed in bfloat16 or wider, within the bound.
A program may use at most 192 MiB of HBM per device.

```python
import math
import jax
import jax.numpy as jnp
import numpy as np
from jax import lax

HEAD_SIZE = 64
STATE = 256
BLOCK = 256
HEADS = 64
GROUPS = 2
SEQUENCE_TOKENS = 2048


def draw_log_decay(key, part):
    random_key_variety, random_key_quick, random_key_gradual, random_key_wobble, random_key_spike, random_key_missing = jax.random.split(key, 6)
    fast_share = 0.5
    fast_heads = jax.random.bernoulli(random_key_variety, fast_share, (HEADS, 1))
    fast_rate = jnp.exp(jax.random.uniform(random_key_quick, (HEADS, 1), jnp.float32, math.log(1.0 / 50.0), math.log(1.0 / 30.0)))
    slow_rate = math.log(2.5) / SEQUENCE_TOKENS * jax.random.uniform(random_key_gradual, (HEADS, 1), jnp.float32, 0.5, 1.0)
    baseline_rate = jnp.where(fast_heads, fast_rate, slow_rate)
    random_wobble = jnp.exp(jax.random.uniform(random_key_wobble, (HEADS, SEQUENCE_TOKENS), jnp.float32, math.log(0.5), math.log(2.0)))
    spike_locations = jax.random.randint(random_key_spike, (2,), 0, SEQUENCE_TOKENS)
    token_places = jnp.arange(SEQUENCE_TOKENS)
    spike_mask = jnp.any(token_places[None, :] == spike_locations[:, None], axis=0)
    missing_fraction = jax.random.uniform(random_key_missing, (HEADS, SEQUENCE_TOKENS), jnp.float32, 0.2, 0.5)
    spike_decrease = jnp.where(spike_mask[None, :], jnp.log(1.0 - missing_fraction), 0.0)
    return (spike_decrease - baseline_rate * random_wobble).astype(jnp.float32)


def levels(rng, shape, shards, least, high):
    factor_of = 1.0
    for axis_at, blocks in shards:
        draws = jax.random.uniform(jax.random.fold_in(jax.random.fold_in(rng, 6), axis_at), (blocks,), jnp.float32, least / len(shards), high / len(shards))
        factor_of = factor_of * jnp.repeat(jnp.exp(draws), shape[axis_at] // blocks).reshape((-1,) + (1,) * (len(shape) - 1 - axis_at))
    return factor_of


def split_up(amount, total, bound, slope):
    weights = [(1 << 20) // math.isqrt(rank ** slope) + 1 for rank in range(2, amount + 1)]
    spare, counts = total - bound - (amount - 1), [1] * (amount - 1)
    while spare > 0:
        candidates = [i for i in range(amount - 1) if counts[i] < bound]
        whole, budget = sum([weights[i] for i in candidates]), spare
        for i in candidates:
            extra = min(bound - counts[i], max(1, budget * weights[i] // whole), spare)
            counts[i] = counts[i] + extra
            spare = spare - extra
    return np.array([bound] + counts)


def uneven_parts(key, amount, total, bound, skew):
    if amount == 2:
        one = jax.random.randint(key, (), max(1, total - bound), min(bound, total - 1) + 1)
        return jnp.stack([one, total - one])
    tallies = jnp.asarray(split_up(amount, total, bound, skew), jnp.int32)
    couples = (amount - 1) // 2
    giver, receiver = tallies[1:1 + 2 * couples:2], tallies[2:2 + 2 * couples:2]
    slack = jnp.minimum(giver - 1, bound - receiver)
    shifted = jax.random.randint(jax.random.fold_in(key, 1), (couples,), 0, 1 << 20) % (slack + 1)
    tallies = tallies.at[1:1 + 2 * couples:2].set(giver - shifted).at[2:2 + 2 * couples:2].set(receiver + shifted)
    return tallies[jax.random.permutation(jax.random.fold_in(key, 2), amount)]


def gaussian(key, extent, deviation, bound, cuts=(), kind=jnp.bfloat16):
    entries = jax.random.normal(key, extent, jnp.float32) * deviation
    if len(cuts) > 0:
        entries = levels(key, extent, cuts, -0.22, 0.18) * entries
    return jnp.clip(entries, min=-bound, max=bound).astype(kind)


def setup_inputs(seed: int = 0) -> dict:
    key_of = jax.random.split(jax.random.key(seed), 8)
    return {
        "inputs": gaussian(key_of[0], (SEQUENCE_TOKENS, HEADS * HEAD_SIZE), 1.0, 6.0, ((0, 8), (1, 4))),
        "log_decay": draw_log_decay(jax.random.fold_in(key_of[7], 71), 0),
        "in_b": gaussian(key_of[2], (SEQUENCE_TOKENS, GROUPS * STATE), 0.035, 0.20996094, ((0, 8), (1, 4))),
        "in_c": gaussian(key_of[3], (SEQUENCE_TOKENS, GROUPS * STATE), 0.035, 0.20996094, ((0, 8), (1, 4))),
        "seg_ids": jnp.searchsorted(jnp.cumsum(uneven_parts(key_of[4], 6, SEQUENCE_TOKENS, SEQUENCE_TOKENS // 2, 0)), jnp.arange(SEQUENCE_TOKENS), side="right").astype(jnp.int32),
        "skip_gain": jnp.clip(1.0 + 0.18 * jax.random.normal(key_of[5], (HEADS,), jnp.float32), 0.1, 1.9),
        "grad_out": gaussian(key_of[6], (SEQUENCE_TOKENS, HEADS * HEAD_SIZE), 0.02, 0.119628906, ((0, 8), (1, 4))),
    }


highest = lax.Precision.HIGHEST


def block_tables(decay_rows, seg_block, prev_seg):
    cum_decay = jnp.cumsum(decay_rows, axis=-1)
    total_decay = cum_decay[..., -1]
    last_seg = seg_block[-1]
    row_index = jnp.arange(seg_block.shape[0])
    keep_mask = (row_index[:, None] >= row_index[None, :]) & (seg_block[:, None] == seg_block[None, :])
    decay_table = jnp.exp(jnp.where(keep_mask, cum_decay[..., :, None] - cum_decay[..., None, :], -jnp.inf))
    start_weight = jnp.exp(cum_decay) * (seg_block == prev_seg).astype(cum_decay.dtype)
    end_weight = jnp.exp(total_decay[..., None] - cum_decay) * (seg_block == last_seg).astype(cum_decay.dtype)
    carry_gain = jnp.exp(total_decay) * (last_seg == prev_seg).astype(cum_decay.dtype)
    return decay_table, start_weight, end_weight, carry_gain, last_seg


def block_mix(decay_table, b_float, c_float):
    score = jnp.einsum('ign,jgn->gij', c_float, b_float, precision=highest)
    return (decay_table * score[:, None]).astype(jnp.bfloat16).astype(jnp.float32)


def reference(inputs, log_decay, in_b, in_c, seg_ids, skip_gain, grad_out):
    per_group = HEADS // GROUPS
    block_total = SEQUENCE_TOKENS // BLOCK
    input_blocks = inputs.reshape(block_total, BLOCK, GROUPS, per_group, HEAD_SIZE)
    grad_blocks = grad_out.reshape(block_total, BLOCK, GROUPS, per_group, HEAD_SIZE)
    decay_blocks = log_decay.reshape(GROUPS, per_group, block_total, BLOCK).transpose(2, 0, 1, 3)
    seg_blocks = seg_ids.reshape(block_total, BLOCK)
    b_blocks = in_b.reshape(block_total, BLOCK, GROUPS, STATE)
    c_blocks = in_c.reshape(block_total, BLOCK, GROUPS, STATE)
    gains = skip_gain.reshape(GROUPS, per_group)

    def forward_block(carried, block):
        state_now, prev_seg = carried
        x_block, decay_rows, seg_block, b_block, c_block = block
        decay_table, start_weight, end_weight, carry_gain, last_seg = block_tables(decay_rows, seg_block, prev_seg)
        b_float = b_block.astype(jnp.float32)
        c_float = c_block.astype(jnp.float32)
        x_float = x_block.astype(jnp.float32)
        mixed = block_mix(decay_table, b_float, c_float)
        inner_term = jnp.einsum('ghij,jghp->ighp', mixed, x_float, precision=highest)
        outer_term = jnp.einsum('ign,ghpn->ighp', c_float, state_now, precision=highest)
        outer_term = outer_term * jnp.transpose(start_weight, (2, 0, 1))[..., None]
        weighted = x_float * jnp.transpose(end_weight, (2, 0, 1))[..., None]
        fresh_state = jnp.einsum('jghp,jgn->ghpn', weighted, b_float, precision=highest)
        next_state = carry_gain[..., None, None] * state_now + fresh_state
        return (next_state, last_seg), (inner_term + outer_term, state_now, prev_seg)

    start_state = jnp.zeros((GROUPS, per_group, HEAD_SIZE, STATE), jnp.float32)
    start_seg = jnp.array(-1, seg_ids.dtype)
    _, (scan_terms, entering, prev_segs) = lax.scan(
        forward_block, (start_state, start_seg), (input_blocks, decay_blocks, seg_blocks, b_blocks, c_blocks))
    x_all = input_blocks.astype(jnp.float32)
    ssd_out = (scan_terms + gains[None, None, :, :, None] * x_all).astype(jnp.bfloat16)
    ssd_out = ssd_out.reshape(SEQUENCE_TOKENS, HEADS * HEAD_SIZE)

    def backward_block(adjoint, block):
        x_block, decay_rows, seg_block, b_block, c_block, grad_block, state_now, prev_seg = block
        decay_table, start_weight, end_weight, carry_gain, last_seg = block_tables(decay_rows, seg_block, prev_seg)
        b_float = b_block.astype(jnp.float32)
        c_float = c_block.astype(jnp.float32)
        x_float = x_block.astype(jnp.float32)
        grad_float = grad_block.astype(jnp.float32)
        mixed = block_mix(decay_table, b_float, c_float)
        end_t = jnp.transpose(end_weight, (2, 0, 1))[..., None]
        start_t = jnp.transpose(start_weight, (2, 0, 1))[..., None]
        grad_inputs = jnp.einsum('ghij,ighp->jghp', mixed, grad_float, precision=highest)
        grad_inputs = grad_inputs + jnp.einsum('jgn,ghpn->jghp', b_float, adjoint, precision=highest) * end_t
        grad_mix = jnp.einsum('ighp,jghp->ghij', grad_float, x_float, precision=highest)
        dscore = jnp.sum(grad_mix * decay_table, axis=1)
        grad_bmap = jnp.einsum('gij,ign->jgn', dscore, c_float, precision=highest)
        grad_bmap = grad_bmap + jnp.einsum('jghp,ghpn->jgn', x_float * end_t, adjoint, precision=highest)
        grad_cmap = jnp.einsum('gij,jgn->ign', dscore, b_float, precision=highest)
        grad_start = grad_float * start_t
        grad_cmap = grad_cmap + jnp.einsum('ighp,ghpn->ign', grad_start, state_now, precision=highest)
        back_state = jnp.einsum('ighp,ign->ghpn', grad_start, c_float, precision=highest)
        next_adjoint = back_state + carry_gain[..., None, None] * adjoint
        return next_adjoint, (grad_inputs, grad_bmap, grad_cmap)

    _, (grad_terms, grad_bmaps, grad_cmaps) = lax.scan(
        backward_block, jnp.zeros((GROUPS, per_group, HEAD_SIZE, STATE), jnp.float32),
        (input_blocks, decay_blocks, seg_blocks, b_blocks, c_blocks, grad_blocks, entering, prev_segs),
        reverse=True)
    grad_all = grad_blocks.astype(jnp.float32)
    grad_x = (grad_terms + gains[None, None, :, :, None] * grad_all).astype(jnp.bfloat16)
    grad_x = grad_x.reshape(SEQUENCE_TOKENS, HEADS * HEAD_SIZE)
    grad_b = grad_bmaps.astype(jnp.bfloat16).reshape(SEQUENCE_TOKENS, GROUPS * STATE)
    grad_c = grad_cmaps.astype(jnp.bfloat16).reshape(SEQUENCE_TOKENS, GROUPS * STATE)
    return ssd_out, grad_x, grad_b, grad_c
```

```python
import functools

import jax
import jax.numpy as jnp
from jax import lax
from jax.experimental import pallas as pl
from jax.experimental.pallas import tpu as pltpu
from jax.sharding import PartitionSpec as P

MESH = pl.DeviceIdType.MESH
BF = jnp.bfloat16
F32 = jnp.float32
PARTS = 4
PAD = 16
LOG2E = 1.4426950408889634
VMEM2 = 16 << 20
NT = (((1,), (1,)), ((), ()))
NN = (((1,), (0,)), ((), ()))
TN = (((0,), (0,)), ((), ()))


def mm(a, b, dims=NN):
    return lax.dot_general(a, b, dims, preferred_element_type=F32)


def split(v):
    hi = v.astype(BF)
    return hi, (v - hi.astype(F32)).astype(BF)


def encode(ref, q, way, value):
    n = value.shape[0]
    top = jnp.maximum(jnp.max(jnp.abs(value), axis=0, keepdims=True), 1e-30)
    power = jnp.ceil(jnp.log(top) * LOG2E) - 15.0
    code = jnp.clip(jnp.round(value * jnp.exp2(-power)), -32767.0, 32767.0)
    ref[q, way, 0:n, :] = code.astype(jnp.int32).astype(jnp.int16)
    ref[q, way, n : n + PAD, :] = jnp.broadcast_to(power, (PAD, value.shape[1])).astype(jnp.int32).astype(jnp.int16)


def decode(ref, at, weight):
    n = ref.shape[1] - PAD
    power = ref[at, n : n + PAD, :].astype(jnp.int32).astype(F32)[0:1]
    return ref[at, 0:n, :].astype(jnp.int32).astype(F32) * (weight * jnp.exp2(power))


def kernel(
    peers, x_hbm, ld_hbm, b_hbm, c_hbm, seg_hbm, skip_hbm, d_hbm,
    ssd_ref, gx_ref, gb_ref, gc_ref,
    x_ref, ld_ref, seg_ref, skip_ref, d_ref, in_sem, bc, info, acum_s, acx, we_s, ws_s, wxh, wxl, wdh, wdl, bias, score_s, dsc,
    ssd_acc, gx_acc, fg, full, half, tbuf, slots, st, gacc, grecv,
    bc_send, bc_recv, i_send, i_recv, d_send, d_recv, t_send, t_recv, s_send, s_recv, g_send, g_recv,
):
    tokens, width = x_hbm.shape
    heads = ld_hbm.shape[0]
    head = width // heads
    hw = width // 2
    pairs = width // 128
    chips = peers // 2
    me = lax.axis_index("ctx")
    hd = lax.axis_index("head")
    side = hd % 2
    mate = hd + 1 - 2 * side
    core = me % 2
    chip = me // 2
    sib = me + 1 - 2 * core

    inputs = [
        pltpu.make_async_copy(src, dst, in_sem.at[k])
        for k, (src, dst) in enumerate((
            (ld_hbm, ld_ref), (seg_hbm, seg_ref), (x_hbm, x_ref), (d_hbm, d_ref), (skip_hbm, skip_ref),
            (b_hbm, bc.at[0, side]), (c_hbm, bc.at[1, side])))
    ]
    for copy in inputs:
        copy.start()

    barrier = pltpu.get_barrier_semaphore()
    for off in range(1, peers):
        pl.semaphore_signal(barrier, inc=1, device_id={"ctx": me ^ off}, device_id_type=MESH)
    pl.semaphore_signal(barrier, inc=1, device_id={"head": mate}, device_id_type=MESH)

    low = lax.broadcasted_iota(jnp.int32, (1, 128), 1) < head
    rows = lax.broadcasted_iota(jnp.int32, (tokens, tokens), 0)
    cols = lax.broadcasted_iota(jnp.int32, (tokens, tokens), 1)
    ones = jnp.where(rows <= cols, 1.0, 0.0).astype(BF)
    inputs[0].wait()
    ld = ld_ref[...]
    l0 = ld.astype(BF)
    r1 = ld - l0.astype(F32)
    l1 = r1.astype(BF)
    l2 = (r1 - l1.astype(F32)).astype(BF)
    acum = mm(l0, ones) + mm(l1, ones) + mm(l2, ones)
    acum_s[...] = acum
    acum_t = jnp.concatenate([acum, jnp.zeros((128 - heads, tokens), F32)], axis=0).T
    for p in range(pairs):
        acx[:, p * 128 : (p + 1) * 128] = jnp.where(
            low, acum_t[:, 2 * p : 2 * p + 1], acum_t[:, 2 * p + 1 : 2 * p + 2]
        )
    inputs[1].wait()
    seg_row = seg_ref[...].astype(F32)
    seg_col = jnp.broadcast_to(seg_row, (128, tokens)).T
    last = jnp.broadcast_to(seg_row[:, tokens - 1 : tokens], (1, hw))
    info[me, 0:1, :] = acx[tokens - 1 : tokens, 0:hw]
    info[me, 1:2, :] = acx[tokens - 1 : tokens, hw:width]
    info[me, 2:3, :] = last
    info[me, 3:4, :] = jnp.broadcast_to(seg_row[:, 0:1], (1, hw))

    inputs[2].wait()
    end_mask = jnp.where(seg_col == last[:, 0:128], 1.0, 0.0)
    for p in range(pairs):
        s = slice(p * 128, (p + 1) * 128)
        a = acx[:, s]
        we = jnp.exp(a[tokens - 1 : tokens, :] - a) * end_mask
        we_s[:, s] = we
        hi, lo = split(x_ref[:, s].astype(F32) * we)
        wxh[:, s] = hi
        wxl[:, s] = lo

    pl.semaphore_wait(barrier, peers)

    bc_copies = []
    for k, ref in enumerate((b_hbm, c_hbm)):
        copy = pltpu.make_async_remote_copy(
            src_ref=ref, dst_ref=bc.at[k, side], send_sem=bc_send.at[k], recv_sem=bc_recv.at[k],
            device_id={"head": mate}, device_id_type=MESH)
        copy.start()
        bc_copies.append(copy)
    i_copies = []
    for off in range(1, peers):
        copy = pltpu.make_async_remote_copy(
            src_ref=info.at[me], dst_ref=info.at[me], send_sem=i_send.at[off - 1], recv_sem=i_recv.at[off - 1],
            device_id={"ctx": me ^ off}, device_id_type=MESH)
        copy.start()
        i_copies.append(copy)

    def info_wait(off):
        src = me ^ off
        pltpu.make_async_remote_copy(
            src_ref=info.at[src], dst_ref=info.at[src], send_sem=i_send.at[off - 1], recv_sem=i_recv.at[off - 1],
            device_id={"ctx": src}, device_id_type=MESH).wait_recv()

    def seg_last(i):
        return info[i, 2:3, :]

    def seg_first(i):
        return info[i, 3:4, :]

    inputs[3].wait()
    start_mask = jnp.where(seg_col == seg_row[:, 0:1], 1.0, 0.0)
    for p in range(pairs):
        s = slice(p * 128, (p + 1) * 128)
        ws = jnp.exp(acx[:, s]) * start_mask
        ws_s[:, s] = ws
        hi, lo = split(d_ref[:, s].astype(F32) * ws)
        wdh[:, s] = hi
        wdl[:, s] = lo

    for copy in bc_copies:
        copy.wait_recv()
    inputs[5].wait()
    inputs[6].wait()
    b_full = jnp.concatenate([bc[0, 0], bc[0, 1]], axis=1)
    c_full = jnp.concatenate([bc[1, 0], bc[1, 1]], axis=1)
    b_t = b_full.T
    c_t = c_full.T
    info_wait(1)
    joined = jnp.where(seg_first(2 * chip + 1) == seg_last(2 * chip), 1.0, 0.0)

    def carry(i, k):
        return jnp.exp(info[i, pl.ds(k, 1), :]) * jnp.where(seg_first(i) == seg_last(i), joined, 0.0)

    parts = fg.shape[0]
    cw = fg.shape[4]
    sib_carry = carry(sib, core)
    my_carry = carry(me, core)
    d_copies = []
    t_copies = []

    def forward(q):
        u = slice(q * cw, (q + 1) * cw)
        d_copies[2 * q].wait_recv()
        encode(tbuf, q, core, half[q] + sib_carry[:, u] * fg[q, core, core])
        d_copies[2 * q + 1].wait_recv()
        encode(tbuf, q, 1 - core, fg[q, 1 - core, core] + my_carry[:, u] * full[q, core])
        for off in range(1, chips):
            other = chip ^ off
            at = q * (chips - 1) + off - 1
            copy = pltpu.make_async_remote_copy(
                src_ref=tbuf.at[q, jnp.where(other > chip, 0, 1)], dst_ref=slots.at[at],
                send_sem=t_send.at[at], recv_sem=t_recv.at[at],
                device_id={"ctx": other * 2 + core}, device_id_type=MESH)
            copy.start()
            t_copies.append(copy)

    for q in range(parts):
        for k in range(2):
            s = slice(k * hw + q * cw, k * hw + (q + 1) * cw)
            fg[q, 0, k] = mm(b_t, wxh[:, s]) + mm(b_t, wxl[:, s])
            fg[q, 1, k] = mm(c_t, wdh[:, s]) + mm(c_t, wdl[:, s])
        half_copy = pltpu.make_async_remote_copy(
            src_ref=fg.at[q, 1 - core, 1 - core], dst_ref=half.at[q],
            send_sem=d_send.at[2 * q], recv_sem=d_recv.at[2 * q],
            device_id={"ctx": sib}, device_id_type=MESH)
        half_copy.start()
        full_copy = pltpu.make_async_remote_copy(
            src_ref=fg.at[q, core], dst_ref=full.at[q],
            send_sem=d_send.at[2 * q + 1], recv_sem=d_recv.at[2 * q + 1],
            device_id={"ctx": sib}, device_id_type=MESH)
        full_copy.start()
        d_copies += [half_copy, full_copy]
        if q:
            forward(q - 1)
    forward(parts - 1)


    bias[...] = jnp.where(
        (rows >= cols) & (jnp.concatenate([seg_col] * (tokens // 128), axis=1) == seg_row), 0.0, -1e30
    )
    inputs[4].wait()
    score_s[...] = mm(c_full, b_full, NT)
    dsc[...] = jnp.zeros_like(dsc)

    def pair_step(p, carried):
        s = pl.ds(pl.multiple_of(p * 128, 128), 128)
        x = x_ref[:, s]
        d = d_ref[:, s]
        gain = jnp.where(low, skip_ref[2 * p], skip_ref[2 * p + 1])
        out = gain * x.astype(F32)
        gx = gain * d.astype(F32)
        zero = jnp.zeros_like(x)
        total = dsc[...]
        for k in range(2):
            mine = low if k == 0 else jnp.logical_not(low)
            xm = jnp.where(mine, x, zero)
            dm = jnp.where(mine, d, zero)
            a_col = acx[:, s][:, k * head : k * head + 1]
            a_row = acum_s[pl.ds(2 * p + k, 1), :]
            table = jnp.exp((a_col - a_row) + bias[...])
            mixed = (table * score_s[...]).astype(BF)
            out = out + mm(mixed, xm)
            gx = gx + mm(mixed, dm, TN)
            total = total + mm(dm, x, NT) * table
        dsc[...] = total
        ssd_acc[:, s] = out
        gx_acc[:, s] = gx
        return carried

    lax.fori_loop(0, pairs, pair_step, 0)

    ds_hi, ds_lo = split(dsc[...])
    gb = mm(ds_hi, c_full, TN) + mm(ds_lo, c_full, TN)
    gc = mm(ds_hi, b_full) + mm(ds_lo, b_full)

    for off in range(2, peers):
        info_wait(off)
    weights = []
    for off in range(1, chips):
        src = chip ^ off
        first = jnp.minimum(src, chip)
        final = jnp.maximum(src, chip)
        total = jnp.zeros((1, hw), F32)
        for i in range(peers):
            within = (i >= 2 * first + 2) & (i < 2 * final)
            total = total + jnp.where(within, info[i, pl.ds(core, 1), :], 0.0)
        weights.append(jnp.exp(total) * jnp.where(seg_last(2 * first + 1) == seg_first(2 * final), 1.0, 0.0))
    sib_both = [carry(sib, k) for k in range(2)]

    def gather(q):
        u = slice(q * cw, (q + 1) * cw)
        st[q, core, 0] = jnp.zeros(st.shape[3:], F32)
        st[q, core, 1] = jnp.zeros(st.shape[3:], F32)
        for off in range(1, chips):
            later = jnp.where((chip ^ off) < chip, 0, 1)
            at = q * (chips - 1) + off - 1
            t_copies[at].wait_recv()
            st[q, core, later] = st[q, core, later] + decode(slots, at, weights[off - 1][:, u])
        copy = pltpu.make_async_remote_copy(
            src_ref=st.at[q, core], dst_ref=st.at[q, core], send_sem=s_send.at[q], recv_sem=s_recv.at[q],
            device_id={"ctx": sib}, device_id_type=MESH)
        copy.start()
        return copy

    n = b_full.shape[1] // 2
    g_copies = []

    def send_off(which, grad):
        for k in range(2):
            gacc[k, which] = grad[:, k * n : (k + 1) * n]
        g_copy = pltpu.make_async_remote_copy(
            src_ref=gacc.at[1 - side, which], dst_ref=grecv.at[which],
            send_sem=g_send.at[which], recv_sem=g_recv.at[which],
            device_id={"head": mate}, device_id_type=MESH)
        g_copy.start()
        g_copies.append(g_copy)

    def absorb(q, copy, gb, gc):
        u = slice(q * cw, (q + 1) * cw)
        copy.wait_send()
        pltpu.make_async_remote_copy(
            src_ref=st.at[q, 1 - core], dst_ref=st.at[q, 1 - core], send_sem=s_send.at[q], recv_sem=s_recv.at[q],
            device_id={"ctx": sib}, device_id_type=MESH).wait_recv()
        for k in range(2):
            s = slice(k * hw + q * cw, k * hw + (q + 1) * cw)
            st[q, k, 1 - core] = sib_both[k][:, u] * st[q, k, 1 - core] + joined[:, u] * full[q, k]
            a_hi, a_lo = split(st[q, k, 1])
            gb = gb + mm(wxh[:, s], a_hi, NT) + mm(wxl[:, s], a_hi, NT) + mm(wxh[:, s], a_lo, NT)
        if q == parts - 1:
            send_off(0, gb)
        for k in range(2):
            s = slice(k * hw + q * cw, k * hw + (q + 1) * cw)
            s_hi, s_lo = split(st[q, k, 0])
            gc = gc + mm(wdh[:, s], s_hi, NT) + mm(wdl[:, s], s_hi, NT) + mm(wdh[:, s], s_lo, NT)
        if q == parts - 1:
            send_off(1, gc)
        return gb, gc

    def outputs(q):
        for k in range(2):
            s = slice(k * hw + q * cw, k * hw + (q + 1) * cw)
            s_hi, s_lo = split(st[q, k, 0])
            a_hi, a_lo = split(st[q, k, 1])
            ssd_ref[:, s] = (ssd_acc[:, s] + ws_s[:, s] * (mm(c_full, s_hi) + mm(c_full, s_lo))).astype(BF)
            gx_ref[:, s] = (gx_acc[:, s] + we_s[:, s] * (mm(b_full, a_hi) + mm(b_full, a_lo))).astype(BF)

    s_copy = gather(0)
    for q in range(parts):
        here = s_copy
        if q + 1 < parts:
            gb, gc = absorb(q, here, gb, gc)
            s_copy = gather(q + 1)
            outputs(q)
        else:
            gb, gc = absorb(q, here, gb, gc)
    outputs(parts - 1)

    g_copies[0].wait_recv()
    gb_ref[...] = (gacc[side, 0] + grecv[0]).astype(BF)
    g_copies[1].wait_recv()
    gc_ref[...] = (gacc[side, 1] + grecv[1]).astype(BF)

    for copy in bc_copies + i_copies + d_copies + t_copies + g_copies:
        copy.wait_send()


def per_device(peers, inputs, log_decay, in_b, in_c, seg_ids, skip_gain, grad_out):
    tokens, width = inputs.shape
    heads = log_decay.shape[0]
    cols = in_b.shape[1]
    n = 2 * cols
    hw = width // 2
    chips = peers // 2
    cw = hw // PARTS
    vm = pl.BlockSpec(memory_space=pltpu.VMEM)
    dma = pltpu.SemaphoreType.DMA
    results = pl.pallas_call(
        functools.partial(kernel, peers),
        out_shape=(
            jax.ShapeDtypeStruct((tokens, width), BF),
            jax.ShapeDtypeStruct((tokens, width), BF),
            jax.ShapeDtypeStruct((tokens, cols), BF),
            jax.ShapeDtypeStruct((tokens, cols), BF),
        ),
        in_specs=[pl.BlockSpec(memory_space=pltpu.HBM)] * 7,
        out_specs=(vm, vm, vm, vm),
        scratch_shapes=[
            pltpu.VMEM((tokens, width), BF),
            pltpu.VMEM((heads, tokens), F32),
            pltpu.VMEM((1, tokens), jnp.int32),
            pltpu.SMEM((heads,), F32),
            pltpu.VMEM((tokens, width), BF),
            dma((7,)),
            pltpu.VMEM((2, 2, tokens, cols), BF),
            pltpu.VMEM((peers, 4, hw), F32),
            pltpu.VMEM((heads, tokens), F32),
            pltpu.VMEM((tokens, width), F32),
            pltpu.VMEM((tokens, width), F32),
            pltpu.VMEM((tokens, width), F32),
            pltpu.VMEM((tokens, width), BF),
            pltpu.VMEM((tokens, width), BF),
            pltpu.VMEM((tokens, width), BF),
            pltpu.VMEM((tokens, width), BF),
            pltpu.VMEM((tokens, tokens), F32),
            pltpu.VMEM((tokens, tokens), F32),
            pltpu.VMEM((tokens, tokens), F32),
            pltpu.VMEM((tokens, width), F32),
            pltpu.VMEM((tokens, width), F32),
            pltpu.VMEM((PARTS, 2, 2, n, cw), F32),
            pltpu.VMEM((PARTS, 2, n, cw), F32),
            pltpu.VMEM((PARTS, n, cw), F32),
            pltpu.VMEM((PARTS, 2, n + PAD, cw), jnp.int16),
            pltpu.VMEM((PARTS * (chips - 1), n + PAD, cw), jnp.int16),
            pltpu.VMEM((PARTS, 2, 2, n, cw), F32),
            pltpu.VMEM((2, 2, tokens, cols), F32),
            pltpu.VMEM((2, tokens, cols), F32),
            dma((2,)),
            dma((2,)),
            dma((peers - 1,)),
            dma((peers - 1,)),
            dma((2 * PARTS,)),
            dma((2 * PARTS,)),
            dma((PARTS * (chips - 1),)),
            dma((PARTS * (chips - 1),)),
            dma((PARTS,)),
            dma((PARTS,)),
            dma((2,)),
            dma((2,)),
        ],
        compiler_params=pltpu.CompilerParams(
            collective_id=0, has_side_effects=True, vmem_limit_bytes=48 << 20
        ),
    )(*[pltpu.with_memory_space_constraint(a, pltpu.HBM) for a in (inputs, log_decay, in_b, in_c, seg_ids.reshape(1, tokens), skip_gain, grad_out)])
    hbm = pl.BlockSpec(memory_space=pltpu.HBM)
    return pl.pallas_call(
        hand_over,
        out_shape=tuple(jax.ShapeDtypeStruct(r.shape, r.dtype) for r in results),
        in_specs=[hbm] * 4,
        out_specs=(hbm,) * 4,
        scratch_shapes=[dma((4,))],
        compiler_params=pltpu.CompilerParams(vmem_limit_bytes=VMEM2),
    )(*results)


def hand_over(a, b, c, d, out_a, out_b, out_c, out_d, sem):
    copies = [
        pltpu.make_async_copy(src, dst, sem.at[k])
        for k, (src, dst) in enumerate(((a, out_a), (b, out_b), (c, out_c), (d, out_d)))
    ]
    for copy in copies:
        copy.start()
    for copy in copies:
        copy.wait()


def solution(mesh):
    return jax.shard_map(
        functools.partial(per_device, mesh.shape["ctx"]),
        mesh=mesh,
        in_specs=(
            P("ctx", "head"),
            P("head", "ctx"),
            P("ctx", "head"),
            P("ctx", "head"),
            P("ctx"),
            P("head"),
            P("ctx", "head"),
        ),
        out_specs=(P("ctx", "head"), P("ctx", "head"), P("ctx", "head"), P("ctx", "head")),
        check_vma=False,
    )
```

```python
import functools

import jax
import jax.numpy as jnp
from jax import lax
from jax.experimental import pallas as pl
from jax.experimental.pallas import tpu as pltpu
from jax.sharding import PartitionSpec as P

MESH = pl.DeviceIdType.MESH
BF = jnp.bfloat16
F32 = jnp.float32
PARTS = 2
EARLY = 2
PAD = 16
LOG2E = 1.4426950408889634
VMEM2 = 16 << 20
NT = (((1,), (1,)), ((), ()))
NN = (((1,), (0,)), ((), ()))
TN = (((0,), (0,)), ((), ()))


def mm(a, b, dims=NN):
    return lax.dot_general(a, b, dims, preferred_element_type=F32)


def split(v):
    hi = v.astype(BF)
    return hi, (v - hi.astype(F32)).astype(BF)


def encode(ref, value):
    rows, width = value.shape
    chunks = width // 128
    top = jnp.maximum(jnp.max(jnp.abs(value), axis=0, keepdims=True), 1e-30)
    power = jnp.ceil(jnp.log(top) * LOG2E) - 15.0
    code = jnp.clip(jnp.round(value * jnp.exp2(-power)), -32767.0, 32767.0).astype(jnp.int32).astype(jnp.int16)
    at = lax.broadcasted_iota(jnp.int32, (PAD, 128), 0)
    scales = jnp.zeros((PAD, 128), F32)
    for j in range(chunks):
        s = slice(j * 128, (j + 1) * 128)
        ref[j * rows : (j + 1) * rows, :] = code[:, s]
        scales = jnp.where(at == j, power[:, s], scales)
    ref[chunks * rows : chunks * rows + PAD, :] = scales.astype(jnp.int32).astype(jnp.int16)


def decode(ref, weight):
    chunks = weight.shape[1] // 128
    rows = (ref.shape[0] - PAD) // chunks
    scales = jnp.exp2(ref[chunks * rows : chunks * rows + PAD, :].astype(jnp.int32).astype(F32))
    parts = []
    for j in range(chunks):
        code = ref[j * rows : (j + 1) * rows, :].astype(jnp.int32).astype(F32)
        parts.append(code * (weight[:, j * 128 : (j + 1) * 128] * scales[j : j + 1, :]))
    return jnp.concatenate(parts, axis=1) if chunks > 1 else parts[0]


def kernel(
    peers, x_hbm, ld_hbm, b_hbm, c_hbm, seg_hbm, skip_hbm, d_hbm,
    ssd_ref, gx_ref, gb_ref, gc_ref,
    x_ref, ld_ref, seg_ref, skip_ref, d_ref, in_sem, bc, info, acum_s, acx, we_s, ws_s, wx, wd, bias, score_s, dsc, tab,
    ssd_acc, gx_acc, fg, full, half, tbuf, slots, st, pieces, gacc, zbuf, zrecv,
    bc_send, bc_recv, i_send, i_recv, d_send, d_recv, t_send, t_recv, s_send, s_recv, g_send, g_recv,
):
    tokens, width = x_hbm.shape
    heads = ld_hbm.shape[0]
    head = width // heads
    hw = width // 2
    pairs = width // 128
    chips = peers // 2
    n = b_hbm.shape[1]
    cw = hw // PARTS
    units = 2 * PARTS
    me = lax.axis_index("ctx")
    hd = lax.axis_index("head")
    mate = hd ^ 1
    core = me & 1
    chip = me // 2
    sib = me ^ 1

    inputs = [
        pltpu.make_async_copy(src, dst, in_sem.at[k])
        for k, (src, dst) in enumerate((
            (ld_hbm, ld_ref), (seg_hbm, seg_ref), (x_hbm, x_ref), (d_hbm, d_ref), (skip_hbm, skip_ref),
            (b_hbm, bc.at[0, 0]), (c_hbm, bc.at[1, 0])))
    ]
    for copy in inputs:
        copy.start()

    barrier = pltpu.get_barrier_semaphore()
    pl.semaphore_signal(barrier, inc=1, device_id={"head": mate}, device_id_type=MESH)
    for off in range(peers - 1, 0, -1):
        pl.semaphore_signal(barrier, inc=1, device_id={"ctx": me ^ off}, device_id_type=MESH)

    low = lax.broadcasted_iota(jnp.int32, (1, 128), 1) < head
    rows = lax.broadcasted_iota(jnp.int32, (tokens, tokens), 0)
    cols = lax.broadcasted_iota(jnp.int32, (tokens, tokens), 1)
    ones = jnp.where(rows <= cols, 1.0, 0.0).astype(BF)
    inputs[0].wait()
    ld = ld_ref[...]
    l0 = ld.astype(BF)
    r1 = ld - l0.astype(F32)
    l1 = r1.astype(BF)
    l2 = (r1 - l1.astype(F32)).astype(BF)
    acum = mm(l0, ones) + mm(l1, ones) + mm(l2, ones)
    acum_s[...] = acum
    acum_t = jnp.concatenate([acum, jnp.zeros((128 - heads, tokens), F32)], axis=0).T
    for p in range(pairs):
        acx[:, p * 128 : (p + 1) * 128] = jnp.where(
            low, acum_t[:, 2 * p : 2 * p + 1], acum_t[:, 2 * p + 1 : 2 * p + 2]
        )
    inputs[1].wait()
    seg_row = seg_ref[...].astype(F32)
    seg_col = jnp.broadcast_to(seg_row, (128, tokens)).T
    last = jnp.broadcast_to(seg_row[:, tokens - 1 : tokens], (1, hw))
    info[me, 0:1, :] = acx[tokens - 1 : tokens, 0:hw]
    info[me, 1:2, :] = acx[tokens - 1 : tokens, hw:width]
    info[me, 2:3, :] = last
    info[me, 3:4, :] = jnp.broadcast_to(seg_row[:, 0:1], (1, hw))

    inputs[2].wait()
    inputs[3].wait()
    end_mask = jnp.where(seg_col == last[:, 0:128], 1.0, 0.0)
    start_mask = jnp.where(seg_col == seg_row[:, 0:1], 1.0, 0.0)
    for p in range(pairs):
        s = slice(p * 128, (p + 1) * 128)
        a = acx[:, s]
        we = jnp.exp(a[tokens - 1 : tokens, :] - a) * end_mask
        we_s[:, s] = we
        wx[0:tokens, s], wx[tokens : 2 * tokens, s] = split(x_ref[:, s].astype(F32) * we)
        ws = jnp.exp(a) * start_mask
        ws_s[:, s] = ws
        wd[0:tokens, s], wd[tokens : 2 * tokens, s] = split(d_ref[:, s].astype(F32) * ws)

    def states(h):
        b_t = bc[0, h].T
        c_t = bc[1, h].T
        b_t = jnp.concatenate([b_t, b_t], axis=1)
        c_t = jnp.concatenate([c_t, c_t], axis=1)
        for q in range(PARTS):
            for k in range(2):
                s = slice(k * hw + q * cw, k * hw + (q + 1) * cw)
                fg[h * PARTS + q, 0, k] = mm(b_t, wx[:, s])
                fg[h * PARTS + q, 1, k] = mm(c_t, wd[:, s])

    inputs[5].wait()
    inputs[6].wait()
    states(0)

    pl.semaphore_wait(barrier, peers)

    bc_copies = []
    for k, ref in enumerate((b_hbm, c_hbm)):
        copy = pltpu.make_async_remote_copy(
            src_ref=ref, dst_ref=bc.at[k, 1], send_sem=bc_send.at[k], recv_sem=bc_recv.at[k],
            device_id={"head": mate}, device_id_type=MESH)
        copy.start()
        bc_copies.append(copy)
    i_copies = []
    d_copies = []

    def tell(off):
        copy = pltpu.make_async_remote_copy(
            src_ref=info.at[me], dst_ref=info.at[me], send_sem=i_send.at[off - 1], recv_sem=i_recv.at[off - 1],
            device_id={"ctx": me ^ off}, device_id_type=MESH)
        copy.start()
        i_copies.append(copy)

    def hear(off):
        src = me ^ off
        pltpu.make_async_remote_copy(
            src_ref=info.at[src], dst_ref=info.at[src], send_sem=i_send.at[off - 1], recv_sem=i_recv.at[off - 1],
            device_id={"ctx": src}, device_id_type=MESH).wait_recv()

    def share(u):
        half_copy = pltpu.make_async_remote_copy(
            src_ref=fg.at[u, 1 - core, 1 - core], dst_ref=half.at[u],
            send_sem=d_send.at[2 * u], recv_sem=d_recv.at[2 * u],
            device_id={"ctx": sib}, device_id_type=MESH)
        half_copy.start()
        full_copy = pltpu.make_async_remote_copy(
            src_ref=fg.at[u, core], dst_ref=full.at[u],
            send_sem=d_send.at[2 * u + 1], recv_sem=d_recv.at[2 * u + 1],
            device_id={"ctx": sib}, device_id_type=MESH)
        full_copy.start()
        d_copies.extend([half_copy, full_copy])

    tell(1)
    for u in range(PARTS):
        share(u)
    for off in range(2, peers):
        tell(off)

    bias[...] = jnp.where(
        (rows >= cols) & (jnp.concatenate([seg_col] * (tokens // 128), axis=1) == seg_row), 0.0, -1e30
    )
    dsc[...] = jnp.zeros_like(dsc)
    inputs[4].wait()

    def seg_last(i):
        return info[i, 2:3, :]

    def seg_first(i):
        return info[i, 3:4, :]

    def table_step(p, carried):
        s = pl.ds(pl.multiple_of(p * 128, 128), 128)
        x = x_ref[:, s]
        d = d_ref[:, s]
        zero = jnp.zeros_like(x)
        total = dsc[...]
        for k in range(2):
            mine = low if k == 0 else jnp.logical_not(low)
            dm = jnp.where(mine, d, zero)
            a_col = acx[:, s][:, k * head : k * head + 1]
            a_row = acum_s[pl.ds(2 * p + k, 1), :]
            table = jnp.exp((a_col - a_row) + bias[...])
            tab[2 * p + k] = table
            total = total + mm(dm, x, NT) * table
        dsc[...] = total
        return carried

    def mix_step(p, carried):
        s = pl.ds(pl.multiple_of(p * 128, 128), 128)
        x = x_ref[:, s]
        d = d_ref[:, s]
        gain = jnp.where(low, skip_ref[2 * p], skip_ref[2 * p + 1])
        out = gain * x.astype(F32)
        gx = gain * d.astype(F32)
        zero = jnp.zeros_like(x)
        for k in range(2):
            mine = low if k == 0 else jnp.logical_not(low)
            mixed = (tab[2 * p + k] * score_s[...]).astype(BF)
            out = out + mm(mixed, jnp.where(mine, x, zero))
            gx = gx + mm(mixed, jnp.where(mine, d, zero), TN)
        ssd_acc[:, s] = out
        gx_acc[:, s] = gx
        return carried

    lax.fori_loop(0, EARLY, table_step, 0)

    hear(1)
    joined = jnp.where(seg_first(2 * chip + 1) == seg_last(2 * chip), 1.0, 0.0)

    def carry(i, k):
        return jnp.exp(info[i, pl.ds(k, 1), :]) * jnp.where(seg_first(i) == seg_last(i), joined, 0.0)

    sib_carry = carry(sib, core)
    my_carry = carry(me, core)
    t_copies = []

    def forward(u):
        c = slice((u % PARTS) * cw, (u % PARTS + 1) * cw)
        d_copies[2 * u].wait_recv()
        encode(tbuf.at[u, core], half[u] + sib_carry[:, c] * fg[u, core, core])
        d_copies[2 * u + 1].wait_recv()
        encode(tbuf.at[u, 1 - core], fg[u, 1 - core, core] + my_carry[:, c] * full[u, core])
        for off in range(1, chips):
            other = chip ^ off
            at = u * (chips - 1) + off - 1
            copy = pltpu.make_async_remote_copy(
                src_ref=tbuf.at[u, jnp.where(other > chip, 0, 1)], dst_ref=slots.at[at],
                send_sem=t_send.at[at], recv_sem=t_recv.at[at],
                device_id={"ctx": other * 2 + core}, device_id_type=MESH)
            copy.start()
            t_copies.append(copy)

    for u in range(PARTS):
        forward(u)
    lax.fori_loop(EARLY, pairs, table_step, 0)

    for copy in bc_copies:
        copy.wait_recv()
    states(1)
    for u in range(PARTS, units):
        share(u)

    b_full = jnp.concatenate([bc[0, 0], bc[0, 1]], axis=1)
    c_full = jnp.concatenate([bc[1, 0], bc[1, 1]], axis=1)
    score_s[...] = mm(c_full, b_full, NT)
    ds_hi, ds_lo = split(dsc[...])
    gb = mm(ds_hi, c_full, TN) + mm(ds_lo, c_full, TN)
    gc = mm(ds_hi, b_full) + mm(ds_lo, b_full)
    for h in range(2):
        gacc[0, h] = gb[:, h * n : (h + 1) * n]
        gacc[1, h] = gc[:, h * n : (h + 1) * n]

    for u in range(PARTS, units):
        forward(u)
    lax.fori_loop(0, pairs, mix_step, 0)

    for off in range(2, peers):
        hear(off)
    weights = []
    for off in range(1, chips):
        src = chip ^ off
        first = jnp.minimum(src, chip)
        final = jnp.maximum(src, chip)
        total = jnp.zeros((1, hw), F32)
        for i in range(peers):
            within = (i >= 2 * first + 2) & (i < 2 * final)
            total = total + jnp.where(within, info[i, pl.ds(core, 1), :], 0.0)
        weights.append(jnp.exp(total) * jnp.where(seg_last(2 * first + 1) == seg_first(2 * final), 1.0, 0.0))
    sib_both = [carry(sib, k) for k in range(2)]

    def gather(u):
        c = slice((u % PARTS) * cw, (u % PARTS + 1) * cw)
        st[u, core, 0] = jnp.zeros(st.shape[3:], F32)
        st[u, core, 1] = jnp.zeros(st.shape[3:], F32)
        for off in range(1, chips):
            later = jnp.where((chip ^ off) < chip, 0, 1)
            at = u * (chips - 1) + off - 1
            t_copies[at].wait_recv()
            st[u, core, later] = st[u, core, later] + decode(slots.at[at], weights[off - 1][:, c])
        copy = pltpu.make_async_remote_copy(
            src_ref=st.at[u, core], dst_ref=st.at[u, core], send_sem=s_send.at[u], recv_sem=s_recv.at[u],
            device_id={"ctx": sib}, device_id_type=MESH)
        copy.start()
        return copy

    g_copies = []

    def send_off(which):
        encode(zbuf.at[which], gacc[which, 1])
        g_copy = pltpu.make_async_remote_copy(
            src_ref=zbuf.at[which], dst_ref=zrecv.at[which],
            send_sem=g_send.at[which], recv_sem=g_recv.at[which],
            device_id={"head": mate}, device_id_type=MESH)
        g_copy.start()
        g_copies.append(g_copy)

    def absorb(u, copy):
        h, q = u // PARTS, u % PARTS
        c = slice(q * cw, (q + 1) * cw)
        copy.wait_send()
        pltpu.make_async_remote_copy(
            src_ref=st.at[u, 1 - core], dst_ref=st.at[u, 1 - core], send_sem=s_send.at[u], recv_sem=s_recv.at[u],
            device_id={"ctx": sib}, device_id_type=MESH).wait_recv()
        for k in range(2):
            st[u, k, 1 - core] = sib_both[k][:, c] * st[u, k, 1 - core] + joined[:, c] * full[u, k]
        for which, way, w in ((0, 1, wx), (1, 0, wd)):
            lhs = []
            rhs = []
            for k in range(2):
                s = slice(k * hw + q * cw, k * hw + (q + 1) * cw)
                hi, lo = split(st[u, k, way])
                pieces[q, way, k, h * n : (h + 1) * n, :] = hi
                pieces[q, way, k, (2 + h) * n : (3 + h) * n, :] = lo
                w_hi = w[0:tokens, s]
                lhs += [w_hi, w[tokens : 2 * tokens, s], w_hi]
                rhs += [hi, hi, lo]
            gacc[which, h] = gacc[which, h] + mm(jnp.concatenate(lhs, axis=1), jnp.concatenate(rhs, axis=1), NT)
            if u == units - 1:
                send_off(which)

    b_two = jnp.concatenate([b_full, b_full], axis=1)
    c_two = jnp.concatenate([c_full, c_full], axis=1)

    def outputs(q):
        for k in range(2):
            s = slice(k * hw + q * cw, k * hw + (q + 1) * cw)
            ssd_ref[:, s] = (ssd_acc[:, s] + ws_s[:, s] * mm(c_two, pieces[q, 0, k])).astype(BF)
            gx_ref[:, s] = (gx_acc[:, s] + we_s[:, s] * mm(b_two, pieces[q, 1, k])).astype(BF)

    s_copy = gather(0)
    for u in range(units):
        here = s_copy
        if u + 1 < units:
            s_copy = gather(u + 1)
        absorb(u, here)
        if u >= PARTS:
            outputs(u - PARTS)

    one = jnp.ones((1, n), F32)
    for which, ref in ((0, gb_ref), (1, gc_ref)):
        g_copies[which].wait_recv()
        ref[...] = (gacc[which, 0] + decode(zrecv.at[which], one)).astype(BF)

    for copy in bc_copies + i_copies + d_copies + t_copies + g_copies:
        copy.wait_send()


def per_device(peers, inputs, log_decay, in_b, in_c, seg_ids, skip_gain, grad_out):
    tokens, width = inputs.shape
    heads = log_decay.shape[0]
    n = in_b.shape[1]
    hw = width // 2
    chips = peers // 2
    cw = hw // PARTS
    units = 2 * PARTS
    coded = n * cw // 128 + PAD
    vm = pl.BlockSpec(memory_space=pltpu.VMEM)
    dma = pltpu.SemaphoreType.DMA
    results = pl.pallas_call(
        functools.partial(kernel, peers),
        out_shape=(
            jax.ShapeDtypeStruct((tokens, width), BF),
            jax.ShapeDtypeStruct((tokens, width), BF),
            jax.ShapeDtypeStruct((tokens, n), BF),
            jax.ShapeDtypeStruct((tokens, n), BF),
        ),
        in_specs=[pl.BlockSpec(memory_space=pltpu.HBM)] * 7,
        out_specs=(vm, vm, vm, vm),
        scratch_shapes=[
            pltpu.VMEM((tokens, width), BF),
            pltpu.VMEM((heads, tokens), F32),
            pltpu.VMEM((1, tokens), jnp.int32),
            pltpu.SMEM((heads,), F32),
            pltpu.VMEM((tokens, width), BF),
            dma((7,)),
            pltpu.VMEM((2, 2, tokens, n), BF),
            pltpu.VMEM((peers, 4, hw), F32),
            pltpu.VMEM((heads, tokens), F32),
            pltpu.VMEM((tokens, width), F32),
            pltpu.VMEM((tokens, width), F32),
            pltpu.VMEM((tokens, width), F32),
            pltpu.VMEM((2 * tokens, width), BF),
            pltpu.VMEM((2 * tokens, width), BF),
            pltpu.VMEM((tokens, tokens), F32),
            pltpu.VMEM((tokens, tokens), F32),
            pltpu.VMEM((tokens, tokens), F32),
            pltpu.VMEM((heads, tokens, tokens), F32),
            pltpu.VMEM((tokens, width), F32),
            pltpu.VMEM((tokens, width), F32),
            pltpu.VMEM((units, 2, 2, n, cw), F32),
            pltpu.VMEM((units, 2, n, cw), F32),
            pltpu.VMEM((units, n, cw), F32),
            pltpu.VMEM((units, 2, coded, 128), jnp.int16),
            pltpu.VMEM((units * (chips - 1), coded, 128), jnp.int16),
            pltpu.VMEM((units, 2, 2, n, cw), F32),
            pltpu.VMEM((PARTS, 2, 2, 4 * n, cw), BF),
            pltpu.VMEM((2, 2, tokens, n), F32),
            pltpu.VMEM((2, tokens * n // 128 + PAD, 128), jnp.int16),
            pltpu.VMEM((2, tokens * n // 128 + PAD, 128), jnp.int16),
            dma((2,)),
            dma((2,)),
            dma((peers - 1,)),
            dma((peers - 1,)),
            dma((2 * units,)),
            dma((2 * units,)),
            dma((units * (chips - 1),)),
            dma((units * (chips - 1),)),
            dma((units,)),
            dma((units,)),
            dma((2,)),
            dma((2,)),
        ],
        compiler_params=pltpu.CompilerParams(
            collective_id=0, has_side_effects=True, vmem_limit_bytes=48 << 20
        ),
    )(*[pltpu.with_memory_space_constraint(a, pltpu.HBM) for a in (inputs, log_decay, in_b, in_c, seg_ids.reshape(1, tokens), skip_gain, grad_out)])
    hbm = pl.BlockSpec(memory_space=pltpu.HBM)
    return pl.pallas_call(
        hand_over,
        out_shape=tuple(jax.ShapeDtypeStruct(r.shape, r.dtype) for r in results),
        in_specs=[hbm] * 4,
        out_specs=(hbm,) * 4,
        scratch_shapes=[dma((4,))],
        compiler_params=pltpu.CompilerParams(vmem_limit_bytes=VMEM2),
    )(*results)


def hand_over(a, b, c, d, out_a, out_b, out_c, out_d, sem):
    copies = [
        pltpu.make_async_copy(src, dst, sem.at[k])
        for k, (src, dst) in enumerate(((a, out_a), (b, out_b), (c, out_c), (d, out_d)))
    ]
    for copy in copies:
        copy.start()
    for copy in copies:
        copy.wait()


def solution(mesh):
    return jax.shard_map(
        functools.partial(per_device, mesh.shape["ctx"]),
        mesh=mesh,
        in_specs=(
            P("ctx", "head"),
            P("head", "ctx"),
            P("ctx", "head"),
            P("ctx", "head"),
            P("ctx"),
            P("head"),
            P("ctx", "head"),
        ),
        out_specs=(P("ctx", "head"), P("ctx", "head"), P("ctx", "head"), P("ctx", "head")),
        check_vma=False,
    )
```

```python
import functools

import jax
import jax.numpy as jnp
from jax import lax
from jax.experimental import pallas as pl
from jax.experimental.pallas import tpu as pltpu
from jax.sharding import PartitionSpec as P

MESH = pl.DeviceIdType.MESH
BF = jnp.bfloat16
F32 = jnp.float32
PARTS = 2
EARLY = 2
PAD = 16
LOG2E = 1.4426950408889634
VMEM2 = 16 << 20
NT = (((1,), (1,)), ((), ()))
NN = (((1,), (0,)), ((), ()))
TN = (((0,), (0,)), ((), ()))


def mm(a, b, dims=NN):
    return lax.dot_general(a, b, dims, preferred_element_type=F32)


def split(v):
    hi = v.astype(BF)
    return hi, (v - hi.astype(F32)).astype(BF)


def encode(ref, value):
    rows, width = value.shape
    chunks = width // 128
    top = jnp.maximum(jnp.max(jnp.abs(value), axis=0, keepdims=True), 1e-30)
    power = jnp.ceil(jnp.log(top) * LOG2E) - 15.0
    code = jnp.clip(jnp.round(value * jnp.exp2(-power)), -32767.0, 32767.0).astype(jnp.int32).astype(jnp.int16)
    at = lax.broadcasted_iota(jnp.int32, (PAD, 128), 0)
    scales = jnp.zeros((PAD, 128), F32)
    for j in range(chunks):
        s = slice(j * 128, (j + 1) * 128)
        ref[j * rows : (j + 1) * rows, :] = code[:, s]
        scales = jnp.where(at == j, power[:, s], scales)
    ref[chunks * rows : chunks * rows + PAD, :] = scales.astype(jnp.int32).astype(jnp.int16)


def decode(ref, weight):
    chunks = weight.shape[1] // 128
    rows = (ref.shape[0] - PAD) // chunks
    scales = jnp.exp2(ref[chunks * rows : chunks * rows + PAD, :].astype(jnp.int32).astype(F32))
    parts = []
    for j in range(chunks):
        code = ref[j * rows : (j + 1) * rows, :].astype(jnp.int32).astype(F32)
        parts.append(code * (weight[:, j * 128 : (j + 1) * 128] * scales[j : j + 1, :]))
    return jnp.concatenate(parts, axis=1) if chunks > 1 else parts[0]


def kernel(
    peers, x_hbm, ld_hbm, b_hbm, c_hbm, seg_hbm, skip_hbm, d_hbm,
    ssd_ref, gx_ref, gb_ref, gc_ref,
    x_ref, ld_ref, seg_ref, skip_ref, d_ref, in_sem, bc, info, acum_s, acx, we_s, ws_s, w2, bias, score_s, dsc, tab,
    ssd_acc, gx_acc, fg, full, half, tbuf, slots, twin, st, pieces, gacc, zbuf, zrecv,
    bc_send, bc_recv, i_send, i_recv, d_send, d_recv, t_send, t_recv, s_send, s_recv, g_send, g_recv, near_sem,
):
    tokens, width = x_hbm.shape
    heads = ld_hbm.shape[0]
    head = width // heads
    hw = width // 2
    pairs = width // 128
    chips = peers // 2
    n = b_hbm.shape[1]
    cw = hw // PARTS
    units = 2 * PARTS
    me = lax.axis_index("ctx")
    hd = lax.axis_index("head")
    mate = hd ^ 1
    core = me & 1
    chip = me // 2
    sib = me ^ 1

    inputs = [
        pltpu.make_async_copy(src, dst, in_sem.at[k])
        for k, (src, dst) in enumerate((
            (ld_hbm, ld_ref), (seg_hbm, seg_ref), (x_hbm, x_ref), (d_hbm, d_ref), (skip_hbm, skip_ref),
            (b_hbm, bc.at[0, 0]), (c_hbm, bc.at[1, 0])))
    ]
    for copy in inputs:
        copy.start()

    barrier = pltpu.get_barrier_semaphore()
    pl.semaphore_signal(barrier, inc=1, device_id={"head": mate}, device_id_type=MESH)
    close = peers == 8
    greeted = (1, 2, 4) if close else range(1, peers)
    for off in greeted:
        pl.semaphore_signal(barrier, inc=1, device_id={"ctx": me ^ off}, device_id_type=MESH)

    low = lax.broadcasted_iota(jnp.int32, (1, 128), 1) < head
    rows = lax.broadcasted_iota(jnp.int32, (tokens, tokens), 0)
    cols = lax.broadcasted_iota(jnp.int32, (tokens, tokens), 1)
    ones = jnp.where(rows <= cols, 1.0, 0.0).astype(BF)
    inputs[0].wait()
    ld = ld_ref[...]
    l0 = ld.astype(BF)
    r1 = ld - l0.astype(F32)
    l1 = r1.astype(BF)
    l2 = (r1 - l1.astype(F32)).astype(BF)
    acum = mm(l0, ones) + mm(l1, ones) + mm(l2, ones)
    acum_s[...] = acum
    acum_t = jnp.concatenate([acum, jnp.zeros((128 - heads, tokens), F32)], axis=0).T
    for p in range(pairs):
        acx[:, p * 128 : (p + 1) * 128] = jnp.where(
            low, acum_t[:, 2 * p : 2 * p + 1], acum_t[:, 2 * p + 1 : 2 * p + 2]
        )
    inputs[1].wait()
    seg_row = seg_ref[...].astype(F32)
    seg_col = jnp.broadcast_to(seg_row, (128, tokens)).T
    last = jnp.broadcast_to(seg_row[:, tokens - 1 : tokens], (1, hw))
    info[me, 0:1, :] = acx[tokens - 1 : tokens, 0:hw]
    info[me, 1:2, :] = acx[tokens - 1 : tokens, hw:width]
    info[me, 2:3, :] = last
    info[me, 3:4, :] = jnp.broadcast_to(seg_row[:, 0:1], (1, hw))

    inputs[2].wait()
    inputs[3].wait()
    end_mask = jnp.where(seg_col == last[:, 0:128], 1.0, 0.0)
    start_mask = jnp.where(seg_col == seg_row[:, 0:1], 1.0, 0.0)
    for p in range(pairs):
        s = slice(p * 128, (p + 1) * 128)
        a = acx[:, s]
        we = jnp.exp(a[tokens - 1 : tokens, :] - a) * end_mask
        we_s[:, s] = we
        w2[1, 0:tokens, s], w2[1, tokens : 2 * tokens, s] = split(x_ref[:, s].astype(F32) * we)
        ws = jnp.exp(a) * start_mask
        ws_s[:, s] = ws
        w2[0, 0:tokens, s], w2[0, tokens : 2 * tokens, s] = split(d_ref[:, s].astype(F32) * ws)

    def states(h):
        b_t = bc[0, h].T
        c_t = bc[1, h].T
        b_t = jnp.concatenate([b_t, b_t], axis=1)
        c_t = jnp.concatenate([c_t, c_t], axis=1)
        for q in range(PARTS):
            for k in range(2):
                s = slice(k * hw + q * cw, k * hw + (q + 1) * cw)
                fg[h * PARTS + q, 0, k] = mm(b_t, w2[1, :, s])
                fg[h * PARTS + q, 1, k] = mm(c_t, w2[0, :, s])
            share(h * PARTS + q)

    inputs[5].wait()
    inputs[6].wait()
    pl.semaphore_wait(barrier, len(greeted) + 1)

    bc_copies = []

    def swap_maps():
        for k in range(2):
            copy = pltpu.make_async_remote_copy(
                src_ref=bc.at[k, 0], dst_ref=bc.at[k, 1], send_sem=bc_send.at[k], recv_sem=bc_recv.at[k],
                device_id={"head": mate}, device_id_type=MESH)
            copy.start()
            bc_copies.append(copy)

    i_copies = []
    d_copies = {}

    def tell(off):
        copy = pltpu.make_async_remote_copy(
            src_ref=info.at[me], dst_ref=info.at[me], send_sem=i_send.at[off - 1], recv_sem=i_recv.at[off - 1],
            device_id={"ctx": me ^ off}, device_id_type=MESH)
        copy.start()
        i_copies.append(copy)

    def hear(off):
        src = me ^ off
        pltpu.make_async_remote_copy(
            src_ref=info.at[src], dst_ref=info.at[src], send_sem=i_send.at[off - 1], recv_sem=i_recv.at[off - 1],
            device_id={"ctx": src}, device_id_type=MESH).wait_recv()

    def give(src, dst, at):
        copy = pltpu.make_async_remote_copy(
            src_ref=src, dst_ref=dst, send_sem=d_send.at[at], recv_sem=d_recv.at[at],
            device_id={"ctx": sib}, device_id_type=MESH)
        copy.start()
        d_copies[at] = copy

    def share(u):
        give(fg.at[u, 1 - core, 1 - core], half.at[u], 3 * u)
        give(fg.at[u, core, 1 - core], full.at[u, 1 - core], 3 * u + 1)

    def share_rest(u):
        give(fg.at[u, core, core], full.at[u, core], 3 * u + 2)

    swap_maps()
    tell(1)
    if close:
        pl.semaphore_signal(near_sem, inc=1, device_id={"ctx": me ^ 2}, device_id_type=MESH)
    states(0)
    if close:
        tell(2)
        tell(4)
        pl.semaphore_wait(near_sem, 1)
        tell(6)
    else:
        for off in range(2, peers):
            tell(off)
    for u in range(PARTS):
        share_rest(u)

    bias[...] = jnp.where(
        (rows >= cols) & (jnp.concatenate([seg_col] * (tokens // 128), axis=1) == seg_row), 0.0, -1e30
    )
    dsc[...] = jnp.zeros_like(dsc)
    inputs[4].wait()

    def seg_last(i):
        return info[i, 2:3, :]

    def seg_first(i):
        return info[i, 3:4, :]

    def table_step(p, carried):
        s = pl.ds(pl.multiple_of(p * 128, 128), 128)
        x = x_ref[:, s]
        d = d_ref[:, s]
        zero = jnp.zeros_like(x)
        total = dsc[...]
        for k in range(2):
            mine = low if k == 0 else jnp.logical_not(low)
            dm = jnp.where(mine, d, zero)
            a_col = acx[:, s][:, k * head : k * head + 1]
            a_row = acum_s[pl.ds(2 * p + k, 1), :]
            table = jnp.exp((a_col - a_row) + bias[...])
            tab[2 * p + k] = table
            total = total + mm(dm, x, NT) * table
        dsc[...] = total
        return carried

    def mix_step(p, carried):
        s = pl.ds(pl.multiple_of(p * 128, 128), 128)
        x = x_ref[:, s]
        d = d_ref[:, s]
        gain = jnp.where(low, skip_ref[2 * p], skip_ref[2 * p + 1])
        out = gain * x.astype(F32)
        gx = gain * d.astype(F32)
        zero = jnp.zeros_like(x)
        for k in range(2):
            mine = low if k == 0 else jnp.logical_not(low)
            mixed = (tab[2 * p + k] * score_s[...]).astype(BF)
            out = out + mm(mixed, jnp.where(mine, x, zero))
            gx = gx + mm(mixed, jnp.where(mine, d, zero), TN)
        ssd_acc[:, s] = out
        gx_acc[:, s] = gx
        return carried

    lax.fori_loop(0, EARLY, table_step, 0)

    hear(1)
    joined = jnp.where(seg_first(2 * chip + 1) == seg_last(2 * chip), 1.0, 0.0)

    def carry(i, k):
        return jnp.exp(info[i, pl.ds(k, 1), :]) * jnp.where(seg_first(i) == seg_last(i), joined, 0.0)

    sib_carry = carry(sib, core)
    my_carry = carry(me, core)
    t_copies = {}

    def code(u):
        c = slice((u % PARTS) * cw, (u % PARTS + 1) * cw)
        d_copies[3 * u].wait_recv()
        encode(tbuf.at[u, core], half[u] + sib_carry[:, c] * fg[u, core, core])
        d_copies[3 * u + 1].wait_recv()
        encode(tbuf.at[u, 1 - core], fg[u, 1 - core, core] + my_carry[:, c] * full[u, core])

    def send(u, offs):
        for off in offs:
            other = chip ^ off
            at = u * (chips - 1) + off - 1
            copy = pltpu.make_async_remote_copy(
                src_ref=tbuf.at[u, jnp.where(other > chip, 0, 1)], dst_ref=slots.at[at],
                send_sem=t_send.at[at], recv_sem=t_recv.at[at],
                device_id={"ctx": other * 2 + core}, device_id_type=MESH)
            copy.start()
            t_copies[at] = copy

    direct = (1, 2) if close else range(1, chips)
    across = (3,) if close else ()

    for u in range(PARTS):
        code(u)
        send(u, direct)
        send(u, across)
    lax.fori_loop(EARLY, pairs, table_step, 0)
    if close:
        for off in (2, 4, 6):
            hear(off)
            copy = pltpu.make_async_remote_copy(
                src_ref=info.at[me ^ off], dst_ref=info.at[me ^ off],
                send_sem=i_send.at[off], recv_sem=i_recv.at[off],
                device_id={"ctx": sib}, device_id_type=MESH)
            copy.start()
            i_copies.append(copy)

    for copy in bc_copies:
        copy.wait_recv()
    states(1)

    for u in range(PARTS, units):
        code(u)
        send(u, direct)
    for u in range(PARTS, units):
        send(u, across)
    for u in range(PARTS, units):
        share_rest(u)

    b_full = jnp.concatenate([bc[0, 0], bc[0, 1]], axis=1)
    c_full = jnp.concatenate([bc[1, 0], bc[1, 1]], axis=1)
    score_s[...] = mm(c_full, b_full, NT)
    ds_hi, ds_lo = split(dsc[...])
    gb = mm(ds_hi, c_full, TN) + mm(ds_lo, c_full, TN)
    gc = mm(ds_hi, b_full) + mm(ds_lo, b_full)
    for h in range(2):
        gacc[0, h] = gb[:, h * n : (h + 1) * n]
        gacc[1, h] = gc[:, h * n : (h + 1) * n]

    lax.fori_loop(0, pairs, mix_step, 0)

    for off in (3, 5, 7) if close else range(2, peers):
        hear(off)
    weights = []
    for off in range(1, chips):
        src = chip ^ off
        first = jnp.minimum(src, chip)
        final = jnp.maximum(src, chip)
        total = [jnp.zeros((1, hw), F32)] * 2
        for i in range(peers):
            within = (i >= 2 * first + 2) & (i < 2 * final)
            for k in range(2):
                total[k] = total[k] + jnp.where(within, info[i, pl.ds(core ^ k, 1), :], 0.0)
        linked = jnp.where(seg_last(2 * first + 1) == seg_first(2 * final), 1.0, 0.0)
        weights.append([jnp.exp(total[k]) * linked for k in range(2)])
    sib_both = [carry(sib, k) for k in range(2)]

    s_copies = {}

    def pass_on(u, offs):
        for off in offs:
            at = u * (chips - 1) + off - 1
            t_copies[at].wait_recv()
            copy = pltpu.make_async_remote_copy(
                src_ref=slots.at[at], dst_ref=twin.at[at], send_sem=s_send.at[at], recv_sem=s_recv.at[at],
                device_id={"ctx": sib}, device_id_type=MESH)
            copy.start()
            s_copies[at] = copy

    def gather(u, offs):
        c = slice((u % PARTS) * cw, (u % PARTS + 1) * cw)
        for k, ref in ((0, slots), (1, twin)):
            for off in offs:
                later = jnp.where((chip ^ off) < chip, 0, 1)
                at = u * (chips - 1) + off - 1
                if k:
                    s_copies[at].wait_recv()
                st[u, core ^ k, later] = st[u, core ^ k, later] + decode(ref.at[at], weights[off - 1][k][:, c])

    g_copies = []

    def send_off(which):
        encode(zbuf.at[which], gacc[which, 1])
        g_copy = pltpu.make_async_remote_copy(
            src_ref=zbuf.at[which], dst_ref=zrecv.at[which],
            send_sem=g_send.at[which], recv_sem=g_recv.at[which],
            device_id={"head": mate}, device_id_type=MESH)
        g_copy.start()
        g_copies.append(g_copy)

    def absorb(u, way):
        h, q = u // PARTS, u % PARTS
        c = slice(q * cw, (q + 1) * cw)
        moved = jnp.full((1, cw), way, jnp.int32) != core
        lhs = []
        rhs = []
        for k in range(2):
            s = slice(k * hw + q * cw, k * hw + (q + 1) * cw)
            keep = jnp.where(moved, sib_both[k][:, c], 1.0)
            add = jnp.where(moved, joined[:, c], 0.0)
            hi, lo = split(keep * st[u, k, way] + add * full[u, k])
            pieces[q, way, k, h * n : (h + 1) * n, :] = hi
            pieces[q, way, k, (2 + h) * n : (3 + h) * n, :] = lo
            w_hi = w2[way, 0:tokens, s]
            lhs += [w_hi, w2[way, tokens : 2 * tokens, s], w_hi]
            rhs += [hi, hi, lo]
        gacc[1 - way, h] = gacc[1 - way, h] + mm(jnp.concatenate(lhs, axis=1), jnp.concatenate(rhs, axis=1), NT)

    b_two = jnp.concatenate([b_full, b_full], axis=1)
    c_two = jnp.concatenate([c_full, c_full], axis=1)

    def outputs(q):
        for k in range(2):
            s = slice(k * hw + q * cw, k * hw + (q + 1) * cw)
            ssd_ref[:, s] = (ssd_acc[:, s] + ws_s[:, s] * mm(c_two, pieces[q, 0, k])).astype(BF)
            gx_ref[:, s] = (gx_acc[:, s] + we_s[:, s] * mm(b_two, pieces[q, 1, k])).astype(BF)

    st[...] = jnp.zeros_like(st)
    early = jnp.where(chip < chips // 2, 0, 1)
    pass_on(0, direct)
    pass_on(0, across)
    for u in range(PARTS):
        if u + 1 < PARTS:
            pass_on(u + 1, direct)
            pass_on(u + 1, across)
        else:
            for v in range(PARTS, units):
                pass_on(v, direct)
        gather(u, direct)
        gather(u, across)
        d_copies[3 * u + 2].wait_recv()
        absorb(u, 1)
        absorb(u, 0)
    for u in range(PARTS, units):
        d_copies[3 * u + 2].wait_recv()
        gather(u, direct)
        absorb(u, early)
    send_off(1 - early)
    for u in range(PARTS, units):
        pass_on(u, across)
        gather(u, across)
        absorb(u, 1 - early)
        if u == units - 1:
            send_off(early)
    for q in range(PARTS):
        outputs(q)

    one = jnp.ones((1, n), F32)
    for copy in g_copies:
        copy.wait_recv()
    for which, ref in ((0, gb_ref), (1, gc_ref)):
        ref[...] = (gacc[which, 0] + decode(zrecv.at[which], one)).astype(BF)

    for copy in bc_copies + i_copies + list(d_copies.values()) + list(t_copies.values()) + list(s_copies.values()) + g_copies:
        copy.wait_send()


def per_device(peers, inputs, log_decay, in_b, in_c, seg_ids, skip_gain, grad_out):
    tokens, width = inputs.shape
    heads = log_decay.shape[0]
    n = in_b.shape[1]
    hw = width // 2
    chips = peers // 2
    cw = hw // PARTS
    units = 2 * PARTS
    coded = n * cw // 128 + PAD
    vm = pl.BlockSpec(memory_space=pltpu.VMEM)
    dma = pltpu.SemaphoreType.DMA
    results = pl.pallas_call(
        functools.partial(kernel, peers),
        out_shape=(
            jax.ShapeDtypeStruct((tokens, width), BF),
            jax.ShapeDtypeStruct((tokens, width), BF),
            jax.ShapeDtypeStruct((tokens, n), BF),
            jax.ShapeDtypeStruct((tokens, n), BF),
        ),
        in_specs=[pl.BlockSpec(memory_space=pltpu.HBM)] * 7,
        out_specs=(vm, vm, vm, vm),
        scratch_shapes=[
            pltpu.VMEM((tokens, width), BF),
            pltpu.VMEM((heads, tokens), F32),
            pltpu.VMEM((1, tokens), jnp.int32),
            pltpu.SMEM((heads,), F32),
            pltpu.VMEM((tokens, width), BF),
            dma((7,)),
            pltpu.VMEM((2, 2, tokens, n), BF),
            pltpu.VMEM((peers, 4, hw), F32),
            pltpu.VMEM((heads, tokens), F32),
            pltpu.VMEM((tokens, width), F32),
            pltpu.VMEM((tokens, width), F32),
            pltpu.VMEM((tokens, width), F32),
            pltpu.VMEM((2, 2 * tokens, width), BF),
            pltpu.VMEM((tokens, tokens), F32),
            pltpu.VMEM((tokens, tokens), F32),
            pltpu.VMEM((tokens, tokens), F32),
            pltpu.VMEM((heads, tokens, tokens), F32),
            pltpu.VMEM((tokens, width), F32),
            pltpu.VMEM((tokens, width), F32),
            pltpu.VMEM((units, 2, 2, n, cw), F32),
            pltpu.VMEM((units, 2, n, cw), F32),
            pltpu.VMEM((units, n, cw), F32),
            pltpu.VMEM((units, 2, coded, 128), jnp.int16),
            pltpu.VMEM((units * (chips - 1), coded, 128), jnp.int16),
            pltpu.VMEM((units * (chips - 1), coded, 128), jnp.int16),
            pltpu.VMEM((units, 2, 2, n, cw), F32),
            pltpu.VMEM((PARTS, 2, 2, 4 * n, cw), BF),
            pltpu.VMEM((2, 2, tokens, n), F32),
            pltpu.VMEM((2, tokens * n // 128 + PAD, 128), jnp.int16),
            pltpu.VMEM((2, tokens * n // 128 + PAD, 128), jnp.int16),
            dma((2,)),
            dma((2,)),
            dma((peers - 1,)),
            dma((peers - 1,)),
            dma((3 * units,)),
            dma((3 * units,)),
            dma((units * (chips - 1),)),
            dma((units * (chips - 1),)),
            dma((units * (chips - 1),)),
            dma((units * (chips - 1),)),
            dma((2,)),
            dma((2,)),
            pltpu.SemaphoreType.REGULAR,
        ],
        compiler_params=pltpu.CompilerParams(
            collective_id=0, has_side_effects=True, vmem_limit_bytes=48 << 20
        ),
    )(*[pltpu.with_memory_space_constraint(a, pltpu.HBM) for a in (inputs, log_decay, in_b, in_c, seg_ids.reshape(1, tokens), skip_gain, grad_out)])
    hbm = pl.BlockSpec(memory_space=pltpu.HBM)
    return pl.pallas_call(
        hand_over,
        out_shape=tuple(jax.ShapeDtypeStruct(r.shape, r.dtype) for r in results),
        in_specs=[hbm] * 4,
        out_specs=(hbm,) * 4,
        scratch_shapes=[dma((4,))],
        compiler_params=pltpu.CompilerParams(vmem_limit_bytes=VMEM2),
    )(*results)


def hand_over(a, b, c, d, out_a, out_b, out_c, out_d, sem):
    copies = [
        pltpu.make_async_copy(src, dst, sem.at[k])
        for k, (src, dst) in enumerate(((a, out_a), (b, out_b), (c, out_c), (d, out_d)))
    ]
    for copy in copies:
        copy.start()
    for copy in copies:
        copy.wait()


def solution(mesh):
    return jax.shard_map(
        functools.partial(per_device, mesh.shape["ctx"]),
        mesh=mesh,
        in_specs=(
            P("ctx", "head"),
            P("head", "ctx"),
            P("ctx", "head"),
            P("ctx", "head"),
            P("ctx"),
            P("head"),
            P("ctx", "head"),
        ),
        out_specs=(P("ctx", "head"), P("ctx", "head"), P("ctx", "head"), P("ctx", "head")),
        check_vma=False,
    )
```

```python
import functools

import jax
import jax.numpy as jnp
from jax import lax
from jax.experimental import pallas as pl
from jax.experimental.pallas import tpu as pltpu
from jax.sharding import PartitionSpec as P

MESH = pl.DeviceIdType.MESH
BF = jnp.bfloat16
F32 = jnp.float32
PARTS = 2
EARLY = 2
MIDDLE = 5
MIXED = 2
PAD = 16
LOG2E = 1.4426950408889634
VMEM2 = 16 << 20
NT = (((1,), (1,)), ((), ()))
NN = (((1,), (0,)), ((), ()))
TN = (((0,), (0,)), ((), ()))


def mm(a, b, dims=NN):
    return lax.dot_general(a, b, dims, preferred_element_type=F32)


def split(v):
    hi = v.astype(BF)
    return hi, (v - hi.astype(F32)).astype(BF)


def encode(ref, value):
    rows, width = value.shape
    chunks = width // 128
    top = jnp.maximum(jnp.max(jnp.abs(value), axis=0, keepdims=True), 1e-30)
    power = jnp.ceil(jnp.log(top) * LOG2E) - 15.0
    code = jnp.clip(jnp.round(value * jnp.exp2(-power)), -32767.0, 32767.0).astype(jnp.int32).astype(jnp.int16)
    at = lax.broadcasted_iota(jnp.int32, (PAD, 128), 0)
    scales = jnp.zeros((PAD, 128), F32)
    for j in range(chunks):
        s = slice(j * 128, (j + 1) * 128)
        ref[j * rows : (j + 1) * rows, :] = code[:, s]
        scales = jnp.where(at == j, power[:, s], scales)
    ref[chunks * rows : chunks * rows + PAD, :] = scales.astype(jnp.int32).astype(jnp.int16)


def decode(ref, weight):
    chunks = weight.shape[1] // 128
    rows = (ref.shape[0] - PAD) // chunks
    scales = jnp.exp2(ref[chunks * rows : chunks * rows + PAD, :].astype(jnp.int32).astype(F32))
    parts = []
    for j in range(chunks):
        code = ref[j * rows : (j + 1) * rows, :].astype(jnp.int32).astype(F32)
        parts.append(code * (weight[:, j * 128 : (j + 1) * 128] * scales[j : j + 1, :]))
    return jnp.concatenate(parts, axis=1) if chunks > 1 else parts[0]


def kernel(
    peers, x_hbm, ld_hbm, b_hbm, c_hbm, seg_hbm, skip_hbm, d_hbm,
    ssd_ref, gx_ref, gb_ref, gc_ref,
    x_ref, ld_ref, seg_ref, skip_ref, d_ref, in_sem, bc, info, acum_s, acx, we_s, ws_s, w2, bias, score_s, dsc, tab,
    ssd_acc, gx_acc, fg, got, tbuf, slots, twin, st, pieces, gacc, zbuf, zrecv,
    bc_send, bc_recv, i_send, i_recv, d_send, d_recv, t_send, t_recv, s_send, s_recv, g_send, g_recv, near_sem,
):
    tokens, width = x_hbm.shape
    heads = ld_hbm.shape[0]
    head = width // heads
    hw = width // 2
    pairs = width // 128
    chips = peers // 2
    n = b_hbm.shape[1]
    cw = hw // PARTS
    units = 2 * PARTS
    me = lax.axis_index("ctx")
    hd = lax.axis_index("head")
    mate = hd ^ 1
    core = me & 1
    chip = me // 2
    sib = me ^ 1
    ahead = jnp.where(chip < chips // 2, 0, 1)
    ways = (ahead, 1 - ahead)
    outer = (chip == 0) | (chip == chips - 1)

    inputs = [
        pltpu.make_async_copy(src, dst, in_sem.at[k])
        for k, (src, dst) in enumerate((
            (ld_hbm, ld_ref), (seg_hbm, seg_ref), (x_hbm, x_ref), (d_hbm, d_ref), (skip_hbm, skip_ref),
            (b_hbm, bc.at[0, 0]), (c_hbm, bc.at[1, 0])))
    ]
    for copy in inputs:
        copy.start()

    barrier = pltpu.get_barrier_semaphore()
    pl.semaphore_signal(barrier, inc=1, device_id={"head": mate}, device_id_type=MESH)
    close = peers == 8
    greeted = (1, 2, 4) if close else range(1, peers)
    for off in greeted:
        pl.semaphore_signal(barrier, inc=1, device_id={"ctx": me ^ off}, device_id_type=MESH)

    low = lax.broadcasted_iota(jnp.int32, (1, 128), 1) < head
    rows = lax.broadcasted_iota(jnp.int32, (tokens, tokens), 0)
    cols = lax.broadcasted_iota(jnp.int32, (tokens, tokens), 1)
    ones = jnp.where(rows <= cols, 1.0, 0.0).astype(BF)
    inputs[0].wait()
    ld = ld_ref[...]
    l0 = ld.astype(BF)
    r1 = ld - l0.astype(F32)
    l1 = r1.astype(BF)
    l2 = (r1 - l1.astype(F32)).astype(BF)
    acum = mm(l0, ones) + mm(l1, ones) + mm(l2, ones)
    acum_s[...] = acum
    acum_t = jnp.concatenate([acum, jnp.zeros((128 - heads, tokens), F32)], axis=0).T
    for p in range(pairs):
        acx[:, p * 128 : (p + 1) * 128] = jnp.where(
            low, acum_t[:, 2 * p : 2 * p + 1], acum_t[:, 2 * p + 1 : 2 * p + 2]
        )
    inputs[1].wait()
    seg_row = seg_ref[...].astype(F32)
    seg_col = jnp.broadcast_to(seg_row, (128, tokens)).T
    last = jnp.broadcast_to(seg_row[:, tokens - 1 : tokens], (1, hw))
    info[me, 0:1, :] = acx[tokens - 1 : tokens, 0:hw]
    info[me, 1:2, :] = acx[tokens - 1 : tokens, hw:width]
    info[me, 2:3, :] = last
    info[me, 3:4, :] = jnp.broadcast_to(seg_row[:, 0:1], (1, hw))

    inputs[2].wait()
    inputs[3].wait()
    end_mask = jnp.where(seg_col == last[:, 0:128], 1.0, 0.0)
    start_mask = jnp.where(seg_col == seg_row[:, 0:1], 1.0, 0.0)
    for p in range(pairs):
        s = slice(p * 128, (p + 1) * 128)
        a = acx[:, s]
        we = jnp.exp(a[tokens - 1 : tokens, :] - a) * end_mask
        we_s[:, s] = we
        w2[1, 0:tokens, s], w2[1, tokens : 2 * tokens, s] = split(x_ref[:, s].astype(F32) * we)
        ws = jnp.exp(a) * start_mask
        ws_s[:, s] = ws
        w2[0, 0:tokens, s], w2[0, tokens : 2 * tokens, s] = split(d_ref[:, s].astype(F32) * ws)

    def states(h, way):
        m_t = bc[way, h].T
        m_t = jnp.concatenate([m_t, m_t], axis=1)
        for u in range(h * PARTS, (h + 1) * PARTS):
            q = u % PARTS
            for k in range(2):
                s = slice(k * hw + q * cw, k * hw + (q + 1) * cw)
                fg[u, way, k] = mm(m_t, w2[1 - way, :, s])
            share(u, way)

    inputs[5].wait()
    inputs[6].wait()
    pl.semaphore_wait(barrier, len(greeted) + 1)

    bc_copies = []

    def swap_maps():
        for k in range(2):
            copy = pltpu.make_async_remote_copy(
                src_ref=bc.at[ways[k], 0], dst_ref=bc.at[ways[k], 1], send_sem=bc_send.at[k], recv_sem=bc_recv.at[k],
                device_id={"head": mate}, device_id_type=MESH)
            copy.start()
            bc_copies.append(copy)

    i_copies = []
    d_copies = {}

    def tell(off):
        copy = pltpu.make_async_remote_copy(
            src_ref=info.at[me], dst_ref=info.at[me], send_sem=i_send.at[off - 1], recv_sem=i_recv.at[off - 1],
            device_id={"ctx": me ^ off}, device_id_type=MESH)
        copy.start()
        i_copies.append(copy)

    def hear(off):
        src = me ^ off
        pltpu.make_async_remote_copy(
            src_ref=info.at[src], dst_ref=info.at[src], send_sem=i_send.at[off - 1], recv_sem=i_recv.at[off - 1],
            device_id={"ctx": src}, device_id_type=MESH).wait_recv()

    def give(src, dst, at):
        copy = pltpu.make_async_remote_copy(
            src_ref=src, dst_ref=dst, send_sem=d_send.at[at], recv_sem=d_recv.at[at],
            device_id={"ctx": sib}, device_id_type=MESH)
        copy.start()
        d_copies[at] = copy

    def share(u, way):
        at = 3 * u + (0 if way is ways[0] else 1)
        give(fg.at[u, way, 1 - core], got.at[u, jnp.where(way == core, 1 - core, 2)], at)

    def share_rest(u):
        give(fg.at[u, core, core], got.at[u, core], 3 * u + 2)

    swap_maps()
    tell(1)
    if close:
        pl.semaphore_signal(near_sem, inc=1, device_id={"ctx": me ^ 2}, device_id_type=MESH)
    for way in ways:
        states(0, way)
    if close:
        tell(2)
        tell(4)
        pl.semaphore_wait(near_sem, 1)
        tell(6)
    else:
        for off in range(2, peers):
            tell(off)
    for u in range(PARTS):
        share_rest(u)

    bias[...] = jnp.where(
        (rows >= cols) & (jnp.concatenate([seg_col] * (tokens // 128), axis=1) == seg_row), 0.0, -1e30
    )
    dsc[...] = jnp.zeros_like(dsc)
    inputs[4].wait()

    def seg_last(i):
        return info[i, 2:3, :]

    def seg_first(i):
        return info[i, 3:4, :]

    def table_step(p, carried):
        s = pl.ds(pl.multiple_of(p * 128, 128), 128)
        x = x_ref[:, s]
        d = d_ref[:, s]
        zero = jnp.zeros_like(x)
        total = dsc[...]
        for k in range(2):
            mine = low if k == 0 else jnp.logical_not(low)
            dm = jnp.where(mine, d, zero)
            a_col = acx[:, s][:, k * head : k * head + 1]
            a_row = acum_s[pl.ds(2 * p + k, 1), :]
            table = jnp.exp((a_col - a_row) + bias[...])
            tab[2 * p + k] = table
            total = total + mm(dm, x, NT) * table
        dsc[...] = total
        return carried

    def mix_step(p, carried):
        s = pl.ds(pl.multiple_of(p * 128, 128), 128)
        x = x_ref[:, s]
        d = d_ref[:, s]
        gain = jnp.where(low, skip_ref[2 * p], skip_ref[2 * p + 1])
        out = gain * x.astype(F32)
        gx = gain * d.astype(F32)
        zero = jnp.zeros_like(x)
        for k in range(2):
            mine = low if k == 0 else jnp.logical_not(low)
            mixed = (tab[2 * p + k] * score_s[...]).astype(BF)
            out = out + mm(mixed, jnp.where(mine, x, zero))
            gx = gx + mm(mixed, jnp.where(mine, d, zero), TN)
        ssd_acc[:, s] = out
        gx_acc[:, s] = gx
        return carried

    lax.fori_loop(0, EARLY, table_step, 0)

    hear(1)
    joined = jnp.where(seg_first(2 * chip + 1) == seg_last(2 * chip), 1.0, 0.0)

    def carry(i, k):
        return jnp.exp(info[i, pl.ds(k, 1), :]) * jnp.where(seg_first(i) == seg_last(i), joined, 0.0)

    sib_carry = carry(sib, core)
    my_carry = carry(me, core)
    t_copies = {}

    def code(u, way):
        c = slice((u % PARTS) * cw, (u % PARTS + 1) * cw)
        d_copies[3 * u + (0 if way is ways[0] else 1)].wait_recv()
        mine = jnp.full((1, cw), way, jnp.int32) == core
        kept = jnp.where(mine, sib_carry[:, c], 1.0)
        added = jnp.where(mine, 1.0, my_carry[:, c])
        encode(tbuf.at[u, way], kept * fg[u, way, core] + added * got[u, jnp.where(way == core, 2, core)])

    def message(u, off):
        other = chip ^ off
        at = u * (chips - 1) + off - 1
        t_copies[at] = pltpu.make_async_remote_copy(
            src_ref=tbuf.at[u, jnp.where(other > chip, 0, 1)], dst_ref=slots.at[at],
            send_sem=t_send.at[at], recv_sem=t_recv.at[at],
            device_id={"ctx": other * 2 + core}, device_id_type=MESH)
        return t_copies[at]

    def send(u, offs):
        for off in offs:
            message(u, off).start()

    direct = (1, 2) if close else range(1, chips)
    across = (3,) if close else ()

    for u in range(PARTS):
        for way in ways:
            code(u, way)
        send(u, direct)
    lax.fori_loop(EARLY, MIDDLE, table_step, 0)
    late_units = range(PARTS, units)
    bc_copies[0].wait_recv()
    states(1, ways[0])
    lax.fori_loop(MIDDLE, pairs, table_step, 0)
    for u in late_units:
        code(u, ways[0])
        if close:
            send(u, across)
            send(u, (2,))
            pl.when(outer)(message(u, 1).start)
    bc_copies[1].wait_recv()
    states(1, ways[1])

    b_full = jnp.concatenate([bc[0, 0], bc[0, 1]], axis=1)
    c_full = jnp.concatenate([bc[1, 0], bc[1, 1]], axis=1)
    score_s[...] = mm(c_full, b_full, NT)
    ds_hi, ds_lo = split(dsc[...])
    gb = mm(ds_hi, c_full, TN) + mm(ds_lo, c_full, TN)
    gc = mm(ds_hi, b_full) + mm(ds_lo, b_full)
    for h in range(2):
        gacc[0, h] = gb[:, h * n : (h + 1) * n]
        gacc[1, h] = gc[:, h * n : (h + 1) * n]

    for u in late_units:
        code(u, ways[1])
        if close:
            pl.when(jnp.logical_not(outer))(message(u, 1).start)
        else:
            send(u, direct)
    for u in range(PARTS):
        send(u, across)
    for u in late_units:
        share_rest(u)

    if close:
        for off in (2, 4, 6):
            hear(off)
            copy = pltpu.make_async_remote_copy(
                src_ref=info.at[me ^ off], dst_ref=info.at[me ^ off],
                send_sem=i_send.at[off], recv_sem=i_recv.at[off],
                device_id={"ctx": sib}, device_id_type=MESH)
            copy.start()
            i_copies.append(copy)

    s_copies = {}

    def pass_on(u, offs):
        for off in offs:
            at = u * (chips - 1) + off - 1
            t_copies[at].wait_recv()
            copy = pltpu.make_async_remote_copy(
                src_ref=slots.at[at], dst_ref=twin.at[at], send_sem=s_send.at[at], recv_sem=s_recv.at[at],
                device_id={"ctx": sib}, device_id_type=MESH)
            copy.start()
            s_copies[at] = copy

    lax.fori_loop(0, MIXED, mix_step, 0)
    for u in range(PARTS):
        pass_on(u, direct)
    lax.fori_loop(MIXED, pairs, mix_step, 0)

    for off in (3, 5, 7) if close else range(2, peers):
        hear(off)
    weights = []
    for off in range(1, chips):
        src = chip ^ off
        first = jnp.minimum(src, chip)
        final = jnp.maximum(src, chip)
        total = [jnp.zeros((1, hw), F32)] * 2
        for i in range(peers):
            within = (i >= 2 * first + 2) & (i < 2 * final)
            for k in range(2):
                total[k] = total[k] + jnp.where(within, info[i, pl.ds(core ^ k, 1), :], 0.0)
        linked = jnp.where(seg_last(2 * first + 1) == seg_first(2 * final), 1.0, 0.0)
        weights.append([jnp.exp(total[k]) * linked for k in range(2)])
    sib_both = [carry(sib, k) for k in range(2)]

    def gather(u, offs):
        c = slice((u % PARTS) * cw, (u % PARTS + 1) * cw)
        for k, ref in ((0, slots), (1, twin)):
            for off in offs:
                later = jnp.where((chip ^ off) < chip, 0, 1)
                at = u * (chips - 1) + off - 1
                if k:
                    s_copies[at].wait_recv()
                st[u, core ^ k, later] = st[u, core ^ k, later] + decode(ref.at[at], weights[off - 1][k][:, c])

    g_copies = []

    def send_off(which):
        encode(zbuf.at[which], gacc[which, 1])
        g_copy = pltpu.make_async_remote_copy(
            src_ref=zbuf.at[which], dst_ref=zrecv.at[which],
            send_sem=g_send.at[which], recv_sem=g_recv.at[which],
            device_id={"head": mate}, device_id_type=MESH)
        g_copy.start()
        g_copies.append(g_copy)

    def absorb(u, way):
        h, q = u // PARTS, u % PARTS
        c = slice(q * cw, (q + 1) * cw)
        moved = jnp.full((1, cw), way, jnp.int32) != core
        lhs = []
        rhs = []
        for k in range(2):
            s = slice(k * hw + q * cw, k * hw + (q + 1) * cw)
            keep = jnp.where(moved, sib_both[k][:, c], 1.0)
            add = jnp.where(moved, joined[:, c], 0.0)
            hi, lo = split(keep * st[u, k, way] + add * got[u, k])
            pieces[q, way, k, h * n : (h + 1) * n, :] = hi
            pieces[q, way, k, (2 + h) * n : (3 + h) * n, :] = lo
            w_hi = w2[way, 0:tokens, s]
            lhs += [w_hi, w2[way, tokens : 2 * tokens, s], w_hi]
            rhs += [hi, hi, lo]
        gacc[1 - way, h] = gacc[1 - way, h] + mm(jnp.concatenate(lhs, axis=1), jnp.concatenate(rhs, axis=1), NT)

    b_two = jnp.concatenate([b_full, b_full], axis=1)
    c_two = jnp.concatenate([c_full, c_full], axis=1)

    def outputs(q):
        for k in range(2):
            s = slice(k * hw + q * cw, k * hw + (q + 1) * cw)
            ssd_ref[:, s] = (ssd_acc[:, s] + ws_s[:, s] * mm(c_two, pieces[q, 0, k])).astype(BF)
            gx_ref[:, s] = (gx_acc[:, s] + we_s[:, s] * mm(b_two, pieces[q, 1, k])).astype(BF)

    st[...] = jnp.zeros_like(st)
    for u in range(PARTS):
        d_copies[3 * u + 2].wait_recv()
        gather(u, direct)
        absorb(u, ways[0])
    for u in late_units:
        pass_on(u, across)
        pass_on(u, direct)
    for u in late_units:
        d_copies[3 * u + 2].wait_recv()
        gather(u, direct)
        absorb(u, ways[0])
    send_off(1 - ways[0])
    for u in late_units:
        gather(u, across)
        absorb(u, ways[1])
    send_off(1 - ways[1])
    for u in range(PARTS):
        pass_on(u, across)
    for u in range(PARTS):
        gather(u, across)
        absorb(u, ways[1])
    for q in range(PARTS):
        outputs(q)

    one = jnp.ones((1, n), F32)
    for copy in g_copies:
        copy.wait_recv()
    for which, ref in ((0, gb_ref), (1, gc_ref)):
        ref[...] = (gacc[which, 0] + decode(zrecv.at[which], one)).astype(BF)

    for copy in bc_copies + i_copies + list(d_copies.values()) + list(t_copies.values()) + list(s_copies.values()) + g_copies:
        copy.wait_send()


def per_device(peers, inputs, log_decay, in_b, in_c, seg_ids, skip_gain, grad_out):
    tokens, width = inputs.shape
    heads = log_decay.shape[0]
    n = in_b.shape[1]
    hw = width // 2
    chips = peers // 2
    cw = hw // PARTS
    units = 2 * PARTS
    coded = n * cw // 128 + PAD
    vm = pl.BlockSpec(memory_space=pltpu.VMEM)
    dma = pltpu.SemaphoreType.DMA
    results = pl.pallas_call(
        functools.partial(kernel, peers),
        out_shape=(
            jax.ShapeDtypeStruct((tokens, width), BF),
            jax.ShapeDtypeStruct((tokens, width), BF),
            jax.ShapeDtypeStruct((tokens, n), BF),
            jax.ShapeDtypeStruct((tokens, n), BF),
        ),
        in_specs=[pl.BlockSpec(memory_space=pltpu.HBM)] * 7,
        out_specs=(vm, vm, vm, vm),
        scratch_shapes=[
            pltpu.VMEM((tokens, width), BF),
            pltpu.VMEM((heads, tokens), F32),
            pltpu.VMEM((1, tokens), jnp.int32),
            pltpu.SMEM((heads,), F32),
            pltpu.VMEM((tokens, width), BF),
            dma((7,)),
            pltpu.VMEM((2, 2, tokens, n), BF),
            pltpu.VMEM((peers, 4, hw), F32),
            pltpu.VMEM((heads, tokens), F32),
            pltpu.VMEM((tokens, width), F32),
            pltpu.VMEM((tokens, width), F32),
            pltpu.VMEM((tokens, width), F32),
            pltpu.VMEM((2, 2 * tokens, width), BF),
            pltpu.VMEM((tokens, tokens), F32),
            pltpu.VMEM((tokens, tokens), F32),
            pltpu.VMEM((tokens, tokens), F32),
            pltpu.VMEM((heads, tokens, tokens), F32),
            pltpu.VMEM((tokens, width), F32),
            pltpu.VMEM((tokens, width), F32),
            pltpu.VMEM((units, 2, 2, n, cw), F32),
            pltpu.VMEM((units, 3, n, cw), F32),
            pltpu.VMEM((units, 2, coded, 128), jnp.int16),
            pltpu.VMEM((units * (chips - 1), coded, 128), jnp.int16),
            pltpu.VMEM((units * (chips - 1), coded, 128), jnp.int16),
            pltpu.VMEM((units, 2, 2, n, cw), F32),
            pltpu.VMEM((PARTS, 2, 2, 4 * n, cw), BF),
            pltpu.VMEM((2, 2, tokens, n), F32),
            pltpu.VMEM((2, tokens * n // 128 + PAD, 128), jnp.int16),
            pltpu.VMEM((2, tokens * n // 128 + PAD, 128), jnp.int16),
            dma((2,)),
            dma((2,)),
            dma((peers - 1,)),
            dma((peers - 1,)),
            dma((3 * units,)),
            dma((3 * units,)),
            dma((units * (chips - 1),)),
            dma((units * (chips - 1),)),
            dma((units * (chips - 1),)),
            dma((units * (chips - 1),)),
            dma((2,)),
            dma((2,)),
            pltpu.SemaphoreType.REGULAR,
        ],
        compiler_params=pltpu.CompilerParams(
            collective_id=0, has_side_effects=True, vmem_limit_bytes=48 << 20
        ),
    )(*[pltpu.with_memory_space_constraint(a, pltpu.HBM) for a in (inputs, log_decay, in_b, in_c, seg_ids.reshape(1, tokens), skip_gain, grad_out)])
    hbm = pl.BlockSpec(memory_space=pltpu.HBM)
    return pl.pallas_call(
        hand_over,
        out_shape=tuple(jax.ShapeDtypeStruct(r.shape, r.dtype) for r in results),
        in_specs=[hbm] * 4,
        out_specs=(hbm,) * 4,
        scratch_shapes=[dma((4,))],
        compiler_params=pltpu.CompilerParams(vmem_limit_bytes=VMEM2),
    )(*results)


def hand_over(a, b, c, d, out_a, out_b, out_c, out_d, sem):
    copies = [
        pltpu.make_async_copy(src, dst, sem.at[k])
        for k, (src, dst) in enumerate(((a, out_a), (b, out_b), (c, out_c), (d, out_d)))
    ]
    for copy in copies:
        copy.start()
    for copy in copies:
        copy.wait()


def solution(mesh):
    return jax.shard_map(
        functools.partial(per_device, mesh.shape["ctx"]),
        mesh=mesh,
        in_specs=(
            P("ctx", "head"),
            P("head", "ctx"),
            P("ctx", "head"),
            P("ctx", "head"),
            P("ctx"),
            P("head"),
            P("ctx", "head"),
        ),
        out_specs=(P("ctx", "head"), P("ctx", "head"), P("ctx", "head"), P("ctx", "head")),
        check_vma=False,
    )
```

```python
import functools

import jax
import jax.numpy as jnp
from jax import lax
from jax.experimental import pallas as pl
from jax.experimental.pallas import tpu as pltpu
from jax.sharding import PartitionSpec as P

MESH = pl.DeviceIdType.MESH
BF = jnp.bfloat16
F32 = jnp.float32
PARTS = 1
EARLY = 2
MIDDLE = 5
MIXED = 2
PAD = 16
LOG2E = 1.4426950408889634
VMEM2 = 16 << 20
NT = (((1,), (1,)), ((), ()))
NN = (((1,), (0,)), ((), ()))
TN = (((0,), (0,)), ((), ()))


def mm(a, b, dims=NN):
    return lax.dot_general(a, b, dims, preferred_element_type=F32)


def split(v):
    hi = v.astype(BF)
    return hi, (v - hi.astype(F32)).astype(BF)


def encode(ref, value):
    rows, width = value.shape
    chunks = width // 128
    top = jnp.maximum(jnp.max(jnp.abs(value), axis=0, keepdims=True), 1e-30)
    power = jnp.ceil(jnp.log(top) * LOG2E) - 15.0
    code = jnp.clip(jnp.round(value * jnp.exp2(-power)), -32767.0, 32767.0).astype(jnp.int32).astype(jnp.int16)
    at = lax.broadcasted_iota(jnp.int32, (PAD, 128), 0)
    scales = jnp.zeros((PAD, 128), F32)
    for j in range(chunks):
        s = slice(j * 128, (j + 1) * 128)
        ref[j * rows : (j + 1) * rows, :] = code[:, s]
        scales = jnp.where(at == j, power[:, s], scales)
    ref[chunks * rows : chunks * rows + PAD, :] = scales.astype(jnp.int32).astype(jnp.int16)


def decode(ref, weight):
    chunks = weight.shape[1] // 128
    rows = (ref.shape[0] - PAD) // chunks
    scales = jnp.exp2(ref[chunks * rows : chunks * rows + PAD, :].astype(jnp.int32).astype(F32))
    parts = []
    for j in range(chunks):
        code = ref[j * rows : (j + 1) * rows, :].astype(jnp.int32).astype(F32)
        parts.append(code * (weight[:, j * 128 : (j + 1) * 128] * scales[j : j + 1, :]))
    return jnp.concatenate(parts, axis=1) if chunks > 1 else parts[0]


def kernel(
    peers, x_hbm, ld_hbm, b_hbm, c_hbm, seg_hbm, skip_hbm, d_hbm,
    ssd_ref, gx_ref, gb_ref, gc_ref,
    x_ref, ld_ref, seg_ref, skip_ref, d_ref, in_sem, bc, info, acum_s, acx, we_s, ws_s, w2, bias, score_s, dsc, tab,
    ssd_acc, gx_acc, fg, got, tbuf, slots, twin, st, pieces, gacc, zbuf, zrecv,
    bc_send, bc_recv, i_send, i_recv, d_send, d_recv, t_send, t_recv, s_send, s_recv, g_send, g_recv, near_sem,
):
    tokens, width = x_hbm.shape
    heads = ld_hbm.shape[0]
    head = width // heads
    hw = width // 2
    pairs = width // 128
    chips = peers // 2
    n = b_hbm.shape[1]
    cw = hw // PARTS
    units = 2 * PARTS
    me = lax.axis_index("ctx")
    hd = lax.axis_index("head")
    mate = hd ^ 1
    core = me & 1
    chip = me // 2
    sib = me ^ 1
    ahead = jnp.where(chip < chips // 2, 0, 1)
    ways = (ahead, 1 - ahead)
    outer = (chip == 0) | (chip == chips - 1)

    inputs = [
        pltpu.make_async_copy(src, dst, in_sem.at[k])
        for k, (src, dst) in enumerate((
            (ld_hbm, ld_ref), (seg_hbm, seg_ref), (x_hbm, x_ref), (d_hbm, d_ref), (skip_hbm, skip_ref),
            (b_hbm, bc.at[0, 0]), (c_hbm, bc.at[1, 0])))
    ]
    for copy in inputs:
        copy.start()

    barrier = pltpu.get_barrier_semaphore()
    pl.semaphore_signal(barrier, inc=1, device_id={"head": mate}, device_id_type=MESH)
    close = peers == 8
    greeted = (1, 2, 4) if close else range(1, peers)
    for off in greeted:
        pl.semaphore_signal(barrier, inc=1, device_id={"ctx": me ^ off}, device_id_type=MESH)

    low = lax.broadcasted_iota(jnp.int32, (1, 128), 1) < head
    rows = lax.broadcasted_iota(jnp.int32, (tokens, tokens), 0)
    cols = lax.broadcasted_iota(jnp.int32, (tokens, tokens), 1)
    ones = jnp.where(rows <= cols, 1.0, 0.0).astype(BF)
    inputs[0].wait()
    ld = ld_ref[...]
    l0 = ld.astype(BF)
    r1 = ld - l0.astype(F32)
    l1 = r1.astype(BF)
    l2 = (r1 - l1.astype(F32)).astype(BF)
    acum = mm(l0, ones) + mm(l1, ones) + mm(l2, ones)
    acum_s[...] = acum
    acum_t = jnp.concatenate([acum, jnp.zeros((128 - heads, tokens), F32)], axis=0).T
    for p in range(pairs):
        acx[:, p * 128 : (p + 1) * 128] = jnp.where(
            low, acum_t[:, 2 * p : 2 * p + 1], acum_t[:, 2 * p + 1 : 2 * p + 2]
        )
    inputs[1].wait()
    seg_row = seg_ref[...].astype(F32)
    seg_col = jnp.broadcast_to(seg_row, (128, tokens)).T
    last = jnp.broadcast_to(seg_row[:, tokens - 1 : tokens], (1, hw))
    info[me, 0:1, :] = acx[tokens - 1 : tokens, 0:hw]
    info[me, 1:2, :] = acx[tokens - 1 : tokens, hw:width]
    info[me, 2:3, :] = last
    info[me, 3:4, :] = jnp.broadcast_to(seg_row[:, 0:1], (1, hw))

    inputs[2].wait()
    inputs[3].wait()
    end_mask = jnp.where(seg_col == last[:, 0:128], 1.0, 0.0)
    start_mask = jnp.where(seg_col == seg_row[:, 0:1], 1.0, 0.0)
    for p in range(pairs):
        s = slice(p * 128, (p + 1) * 128)
        a = acx[:, s]
        we = jnp.exp(a[tokens - 1 : tokens, :] - a) * end_mask
        we_s[:, s] = we
        w2[1, 0:tokens, s], w2[1, tokens : 2 * tokens, s] = split(x_ref[:, s].astype(F32) * we)
        ws = jnp.exp(a) * start_mask
        ws_s[:, s] = ws
        w2[0, 0:tokens, s], w2[0, tokens : 2 * tokens, s] = split(d_ref[:, s].astype(F32) * ws)

    def states(h, way):
        m_t = bc[way, h].T
        m_t = jnp.concatenate([m_t, m_t], axis=1)
        for u in range(h * PARTS, (h + 1) * PARTS):
            q = u % PARTS
            for k in range(2):
                s = slice(k * hw + q * cw, k * hw + (q + 1) * cw)
                fg[u, way, k] = mm(m_t, w2[1 - way, :, s])
            share(u, way)

    inputs[5].wait()
    inputs[6].wait()
    pl.semaphore_wait(barrier, len(greeted) + 1)

    bc_copies = []

    def swap_maps():
        for k in range(2):
            copy = pltpu.make_async_remote_copy(
                src_ref=bc.at[ways[k], 0], dst_ref=bc.at[ways[k], 1], send_sem=bc_send.at[k], recv_sem=bc_recv.at[k],
                device_id={"head": mate}, device_id_type=MESH)
            copy.start()
            bc_copies.append(copy)

    i_copies = []
    d_copies = {}

    def tell(off):
        copy = pltpu.make_async_remote_copy(
            src_ref=info.at[me], dst_ref=info.at[me], send_sem=i_send.at[off - 1], recv_sem=i_recv.at[off - 1],
            device_id={"ctx": me ^ off}, device_id_type=MESH)
        copy.start()
        i_copies.append(copy)

    def hear(off):
        src = me ^ off
        pltpu.make_async_remote_copy(
            src_ref=info.at[src], dst_ref=info.at[src], send_sem=i_send.at[off - 1], recv_sem=i_recv.at[off - 1],
            device_id={"ctx": src}, device_id_type=MESH).wait_recv()

    def give(src, dst, at):
        copy = pltpu.make_async_remote_copy(
            src_ref=src, dst_ref=dst, send_sem=d_send.at[at], recv_sem=d_recv.at[at],
            device_id={"ctx": sib}, device_id_type=MESH)
        copy.start()
        d_copies[at] = copy

    def share(u, way):
        at = 3 * u + (0 if way is ways[0] else 1)
        give(fg.at[u, way, 1 - core], got.at[u, jnp.where(way == core, 1 - core, 2)], at)

    def share_rest(u):
        give(fg.at[u, core, core], got.at[u, core], 3 * u + 2)

    swap_maps()
    tell(1)
    if close:
        pl.semaphore_signal(near_sem, inc=1, device_id={"ctx": me ^ 2}, device_id_type=MESH)
    for way in ways:
        states(0, way)
    if close:
        tell(2)
        tell(4)
        pl.semaphore_wait(near_sem, 1)
        tell(6)
    else:
        for off in range(2, peers):
            tell(off)
    for u in range(PARTS):
        share_rest(u)

    bias[...] = jnp.where(
        (rows >= cols) & (jnp.concatenate([seg_col] * (tokens // 128), axis=1) == seg_row), 0.0, -1e30
    )
    dsc[...] = jnp.zeros_like(dsc)
    inputs[4].wait()

    def seg_last(i):
        return info[i, 2:3, :]

    def seg_first(i):
        return info[i, 3:4, :]

    def table_step(p, carried):
        s = pl.ds(pl.multiple_of(p * 128, 128), 128)
        x = x_ref[:, s]
        d = d_ref[:, s]
        zero = jnp.zeros_like(x)
        total = dsc[...]
        for k in range(2):
            mine = low if k == 0 else jnp.logical_not(low)
            dm = jnp.where(mine, d, zero)
            a_col = acx[:, s][:, k * head : k * head + 1]
            a_row = acum_s[pl.ds(2 * p + k, 1), :]
            table = jnp.exp((a_col - a_row) + bias[...])
            tab[2 * p + k] = table
            total = total + mm(dm, x, NT) * table
        dsc[...] = total
        return carried

    def mix_step(p, carried):
        s = pl.ds(pl.multiple_of(p * 128, 128), 128)
        x = x_ref[:, s]
        d = d_ref[:, s]
        gain = jnp.where(low, skip_ref[2 * p], skip_ref[2 * p + 1])
        out = gain * x.astype(F32)
        gx = gain * d.astype(F32)
        zero = jnp.zeros_like(x)
        for k in range(2):
            mine = low if k == 0 else jnp.logical_not(low)
            mixed = (tab[2 * p + k] * score_s[...]).astype(BF)
            out = out + mm(mixed, jnp.where(mine, x, zero))
            gx = gx + mm(mixed, jnp.where(mine, d, zero), TN)
        ssd_acc[:, s] = out
        gx_acc[:, s] = gx
        return carried

    lax.fori_loop(0, EARLY, table_step, 0)

    hear(1)
    joined = jnp.where(seg_first(2 * chip + 1) == seg_last(2 * chip), 1.0, 0.0)

    def carry(i, k):
        return jnp.exp(info[i, pl.ds(k, 1), :]) * jnp.where(seg_first(i) == seg_last(i), joined, 0.0)

    sib_carry = carry(sib, core)
    my_carry = carry(me, core)
    t_copies = {}

    def code(u, way):
        c = slice((u % PARTS) * cw, (u % PARTS + 1) * cw)
        d_copies[3 * u + (0 if way is ways[0] else 1)].wait_recv()
        mine = jnp.full((1, cw), way, jnp.int32) == core
        kept = jnp.where(mine, sib_carry[:, c], 1.0)
        added = jnp.where(mine, 1.0, my_carry[:, c])
        encode(tbuf.at[u, way], kept * fg[u, way, core] + added * got[u, jnp.where(way == core, 2, core)])

    def message(u, off):
        other = chip ^ off
        at = u * (chips - 1) + off - 1
        t_copies[at] = pltpu.make_async_remote_copy(
            src_ref=tbuf.at[u, jnp.where(other > chip, 0, 1)], dst_ref=slots.at[at],
            send_sem=t_send.at[at], recv_sem=t_recv.at[at],
            device_id={"ctx": other * 2 + core}, device_id_type=MESH)
        return t_copies[at]

    def send(u, offs):
        for off in offs:
            message(u, off).start()

    direct = (1, 2) if close else range(1, chips)
    across = (3,) if close else ()

    for u in range(PARTS):
        for way in ways:
            code(u, way)
        send(u, direct)
    lax.fori_loop(EARLY, MIDDLE, table_step, 0)
    late_units = range(PARTS, units)
    bc_copies[0].wait_recv()
    states(1, ways[0])
    lax.fori_loop(MIDDLE, pairs, table_step, 0)
    for u in late_units:
        code(u, ways[0])
        if close:
            send(u, across)
            send(u, (2,))
            pl.when(outer)(message(u, 1).start)
    bc_copies[1].wait_recv()
    states(1, ways[1])

    b_full = jnp.concatenate([bc[0, 0], bc[0, 1]], axis=1)
    c_full = jnp.concatenate([bc[1, 0], bc[1, 1]], axis=1)
    score_s[...] = mm(c_full, b_full, NT)
    ds_hi, ds_lo = split(dsc[...])
    gb = mm(ds_hi, c_full, TN) + mm(ds_lo, c_full, TN)
    gc = mm(ds_hi, b_full) + mm(ds_lo, b_full)
    for h in range(2):
        gacc[0, h] = gb[:, h * n : (h + 1) * n]
        gacc[1, h] = gc[:, h * n : (h + 1) * n]

    for u in late_units:
        code(u, ways[1])
        if close:
            pl.when(jnp.logical_not(outer))(message(u, 1).start)
        else:
            send(u, direct)
    for u in range(PARTS):
        send(u, across)
    for u in late_units:
        share_rest(u)

    if close:
        for off in (2, 4, 6):
            hear(off)
            copy = pltpu.make_async_remote_copy(
                src_ref=info.at[me ^ off], dst_ref=info.at[me ^ off],
                send_sem=i_send.at[off], recv_sem=i_recv.at[off],
                device_id={"ctx": sib}, device_id_type=MESH)
            copy.start()
            i_copies.append(copy)

    s_copies = {}

    def pass_on(u, offs):
        for off in offs:
            at = u * (chips - 1) + off - 1
            t_copies[at].wait_recv()
            copy = pltpu.make_async_remote_copy(
                src_ref=slots.at[at], dst_ref=twin.at[at], send_sem=s_send.at[at], recv_sem=s_recv.at[at],
                device_id={"ctx": sib}, device_id_type=MESH)
            copy.start()
            s_copies[at] = copy

    lax.fori_loop(0, MIXED, mix_step, 0)
    for u in range(PARTS):
        pass_on(u, direct)
    lax.fori_loop(MIXED, pairs, mix_step, 0)

    for off in (3, 5, 7) if close else range(2, peers):
        hear(off)
    weights = []
    for off in range(1, chips):
        src = chip ^ off
        first = jnp.minimum(src, chip)
        final = jnp.maximum(src, chip)
        total = [jnp.zeros((1, hw), F32)] * 2
        for i in range(peers):
            within = (i >= 2 * first + 2) & (i < 2 * final)
            for k in range(2):
                total[k] = total[k] + jnp.where(within, info[i, pl.ds(core ^ k, 1), :], 0.0)
        linked = jnp.where(seg_last(2 * first + 1) == seg_first(2 * final), 1.0, 0.0)
        weights.append([jnp.exp(total[k]) * linked for k in range(2)])
    sib_both = [carry(sib, k) for k in range(2)]

    def gather(u, offs):
        c = slice((u % PARTS) * cw, (u % PARTS + 1) * cw)
        for k, ref in ((0, slots), (1, twin)):
            for off in offs:
                later = jnp.where((chip ^ off) < chip, 0, 1)
                at = u * (chips - 1) + off - 1
                if k:
                    s_copies[at].wait_recv()
                st[u, core ^ k, later] = st[u, core ^ k, later] + decode(ref.at[at], weights[off - 1][k][:, c])

    g_copies = []

    def send_off(which):
        encode(zbuf.at[which], gacc[which, 1])
        g_copy = pltpu.make_async_remote_copy(
            src_ref=zbuf.at[which], dst_ref=zrecv.at[which],
            send_sem=g_send.at[which], recv_sem=g_recv.at[which],
            device_id={"head": mate}, device_id_type=MESH)
        g_copy.start()
        g_copies.append(g_copy)

    def absorb(u, way):
        h, q = u // PARTS, u % PARTS
        c = slice(q * cw, (q + 1) * cw)
        moved = jnp.full((1, cw), way, jnp.int32) != core
        lhs = []
        rhs = []
        for k in range(2):
            s = slice(k * hw + q * cw, k * hw + (q + 1) * cw)
            keep = jnp.where(moved, sib_both[k][:, c], 1.0)
            add = jnp.where(moved, joined[:, c], 0.0)
            hi, lo = split(keep * st[u, k, way] + add * got[u, k])
            pieces[q, way, k, h * n : (h + 1) * n, :] = hi
            pieces[q, way, k, (2 + h) * n : (3 + h) * n, :] = lo
            w_hi = w2[way, 0:tokens, s]
            lhs += [w_hi, w2[way, tokens : 2 * tokens, s], w_hi]
            rhs += [hi, hi, lo]
        gacc[1 - way, h] = gacc[1 - way, h] + mm(jnp.concatenate(lhs, axis=1), jnp.concatenate(rhs, axis=1), NT)

    b_two = jnp.concatenate([b_full, b_full], axis=1)
    c_two = jnp.concatenate([c_full, c_full], axis=1)

    def outputs(q):
        for k in range(2):
            s = slice(k * hw + q * cw, k * hw + (q + 1) * cw)
            ssd_ref[:, s] = (ssd_acc[:, s] + ws_s[:, s] * mm(c_two, pieces[q, 0, k])).astype(BF)
            gx_ref[:, s] = (gx_acc[:, s] + we_s[:, s] * mm(b_two, pieces[q, 1, k])).astype(BF)

    st[...] = jnp.zeros_like(st)
    for u in range(PARTS):
        d_copies[3 * u + 2].wait_recv()
        gather(u, direct)
        absorb(u, ways[0])
    for u in late_units:
        pass_on(u, across)
        pass_on(u, direct)
    for u in late_units:
        d_copies[3 * u + 2].wait_recv()
        gather(u, direct)
        absorb(u, ways[0])
    send_off(1 - ways[0])
    for u in late_units:
        gather(u, across)
        absorb(u, ways[1])
    send_off(1 - ways[1])
    for u in range(PARTS):
        pass_on(u, across)
    for u in range(PARTS):
        gather(u, across)
        absorb(u, ways[1])
    for q in range(PARTS):
        outputs(q)

    one = jnp.ones((1, n), F32)
    for copy in g_copies:
        copy.wait_recv()
    for which, ref in ((0, gb_ref), (1, gc_ref)):
        ref[...] = (gacc[which, 0] + decode(zrecv.at[which], one)).astype(BF)

    for copy in bc_copies + i_copies + list(d_copies.values()) + list(t_copies.values()) + list(s_copies.values()) + g_copies:
        copy.wait_send()


def per_device(peers, inputs, log_decay, in_b, in_c, seg_ids, skip_gain, grad_out):
    tokens, width = inputs.shape
    heads = log_decay.shape[0]
    n = in_b.shape[1]
    hw = width // 2
    chips = peers // 2
    cw = hw // PARTS
    units = 2 * PARTS
    coded = n * cw // 128 + PAD
    vm = pl.BlockSpec(memory_space=pltpu.VMEM)
    dma = pltpu.SemaphoreType.DMA
    results = pl.pallas_call(
        functools.partial(kernel, peers),
        out_shape=(
            jax.ShapeDtypeStruct((tokens, width), BF),
            jax.ShapeDtypeStruct((tokens, width), BF),
            jax.ShapeDtypeStruct((tokens, n), BF),
            jax.ShapeDtypeStruct((tokens, n), BF),
        ),
        in_specs=[pl.BlockSpec(memory_space=pltpu.HBM)] * 7,
        out_specs=(vm, vm, vm, vm),
        scratch_shapes=[
            pltpu.VMEM((tokens, width), BF),
            pltpu.VMEM((heads, tokens), F32),
            pltpu.VMEM((1, tokens), jnp.int32),
            pltpu.SMEM((heads,), F32),
            pltpu.VMEM((tokens, width), BF),
            dma((7,)),
            pltpu.VMEM((2, 2, tokens, n), BF),
            pltpu.VMEM((peers, 4, hw), F32),
            pltpu.VMEM((heads, tokens), F32),
            pltpu.VMEM((tokens, width), F32),
            pltpu.VMEM((tokens, width), F32),
            pltpu.VMEM((tokens, width), F32),
            pltpu.VMEM((2, 2 * tokens, width), BF),
            pltpu.VMEM((tokens, tokens), F32),
            pltpu.VMEM((tokens, tokens), F32),
            pltpu.VMEM((tokens, tokens), F32),
            pltpu.VMEM((heads, tokens, tokens), F32),
            pltpu.VMEM((tokens, width), F32),
            pltpu.VMEM((tokens, width), F32),
            pltpu.VMEM((units, 2, 2, n, cw), F32),
            pltpu.VMEM((units, 3, n, cw), F32),
            pltpu.VMEM((units, 2, coded, 128), jnp.int16),
            pltpu.VMEM((units * (chips - 1), coded, 128), jnp.int16),
            pltpu.VMEM((units * (chips - 1), coded, 128), jnp.int16),
            pltpu.VMEM((units, 2, 2, n, cw), F32),
            pltpu.VMEM((PARTS, 2, 2, 4 * n, cw), BF),
            pltpu.VMEM((2, 2, tokens, n), F32),
            pltpu.VMEM((2, tokens * n // 128 + PAD, 128), jnp.int16),
            pltpu.VMEM((2, tokens * n // 128 + PAD, 128), jnp.int16),
            dma((2,)),
            dma((2,)),
            dma((peers - 1,)),
            dma((peers - 1,)),
            dma((3 * units,)),
            dma((3 * units,)),
            dma((units * (chips - 1),)),
            dma((units * (chips - 1),)),
            dma((units * (chips - 1),)),
            dma((units * (chips - 1),)),
            dma((2,)),
            dma((2,)),
            pltpu.SemaphoreType.REGULAR,
        ],
        compiler_params=pltpu.CompilerParams(
            collective_id=0, has_side_effects=True, vmem_limit_bytes=48 << 20
        ),
    )(*[pltpu.with_memory_space_constraint(a, pltpu.HBM) for a in (inputs, log_decay, in_b, in_c, seg_ids.reshape(1, tokens), skip_gain, grad_out)])
    hbm = pl.BlockSpec(memory_space=pltpu.HBM)
    return pl.pallas_call(
        hand_over,
        out_shape=tuple(jax.ShapeDtypeStruct(r.shape, r.dtype) for r in results),
        in_specs=[hbm] * 4,
        out_specs=(hbm,) * 4,
        scratch_shapes=[dma((4,))],
        compiler_params=pltpu.CompilerParams(vmem_limit_bytes=VMEM2),
    )(*results)


def hand_over(a, b, c, d, out_a, out_b, out_c, out_d, sem):
    copies = [
        pltpu.make_async_copy(src, dst, sem.at[k])
        for k, (src, dst) in enumerate(((a, out_a), (b, out_b), (c, out_c), (d, out_d)))
    ]
    for copy in copies:
        copy.start()
    for copy in copies:
        copy.wait()


def solution(mesh):
    return jax.shard_map(
        functools.partial(per_device, mesh.shape["ctx"]),
        mesh=mesh,
        in_specs=(
            P("ctx", "head"),
            P("head", "ctx"),
            P("ctx", "head"),
            P("ctx", "head"),
            P("ctx"),
            P("head"),
            P("ctx", "head"),
        ),
        out_specs=(P("ctx", "head"), P("ctx", "head"), P("ctx", "head"), P("ctx", "head")),
        check_vma=False,
    )
```

```python
import functools

import jax
import jax.numpy as jnp
from jax import lax
from jax.experimental import pallas as pl
from jax.experimental.pallas import tpu as pltpu
from jax.sharding import PartitionSpec as P

MESH = pl.DeviceIdType.MESH
BF = jnp.bfloat16
F32 = jnp.float32
PARTS = 1
EARLY = 2
MIDDLE = 8
MIXED = 6
PAD = 16
LOG2E = 1.4426950408889634
VMEM2 = 16 << 20
NT = (((1,), (1,)), ((), ()))
NN = (((1,), (0,)), ((), ()))
TN = (((0,), (0,)), ((), ()))


def mm(a, b, dims=NN):
    return lax.dot_general(a, b, dims, preferred_element_type=F32)


def split(v):
    hi = v.astype(BF)
    return hi, (v - hi.astype(F32)).astype(BF)


def encode(ref, value):
    rows, width = value.shape
    chunks = width // 128
    top = jnp.maximum(jnp.max(jnp.abs(value), axis=0, keepdims=True), 1e-30)
    power = jnp.ceil(jnp.log(top) * LOG2E) - 15.0
    code = jnp.clip(jnp.round(value * jnp.exp2(-power)), -32767.0, 32767.0).astype(jnp.int32).astype(jnp.int16)
    at = lax.broadcasted_iota(jnp.int32, (PAD, 128), 0)
    scales = jnp.zeros((PAD, 128), F32)
    for j in range(chunks):
        s = slice(j * 128, (j + 1) * 128)
        ref[j * rows : (j + 1) * rows, :] = code[:, s]
        scales = jnp.where(at == j, power[:, s], scales)
    ref[chunks * rows : chunks * rows + PAD, :] = scales.astype(jnp.int32).astype(jnp.int16)


def decode(ref, weight):
    chunks = weight.shape[1] // 128
    rows = (ref.shape[0] - PAD) // chunks
    scales = jnp.exp2(ref[chunks * rows : chunks * rows + PAD, :].astype(jnp.int32).astype(F32))
    parts = []
    for j in range(chunks):
        code = ref[j * rows : (j + 1) * rows, :].astype(jnp.int32).astype(F32)
        parts.append(code * (weight[:, j * 128 : (j + 1) * 128] * scales[j : j + 1, :]))
    return jnp.concatenate(parts, axis=1) if chunks > 1 else parts[0]


def kernel(
    peers, x_hbm, ld_hbm, b_hbm, c_hbm, seg_hbm, skip_hbm, d_hbm,
    ssd_ref, gx_ref, gb_ref, gc_ref,
    x_ref, ld_ref, seg_ref, skip_ref, d_ref, in_sem, bc, info, acum_s, acx, we_s, ws_s, w2, bias, score_s, dsc, tab,
    ssd_acc, gx_acc, fg, got, tbuf, slots, twin, st, pieces, gacc, zbuf, zrecv,
    bc_send, bc_recv, i_send, i_recv, d_send, d_recv, t_send, t_recv, s_send, s_recv, g_send, g_recv, near_sem,
):
    tokens, width = x_hbm.shape
    heads = ld_hbm.shape[0]
    head = width // heads
    hw = width // 2
    pairs = width // 128
    chips = peers // 2
    n = b_hbm.shape[1]
    cw = hw // PARTS
    units = 2 * PARTS
    me = lax.axis_index("ctx")
    hd = lax.axis_index("head")
    mate = hd ^ 1
    core = me & 1
    chip = me // 2
    sib = me ^ 1
    ahead = jnp.where(chip < chips // 2, 0, 1)
    ways = (ahead, 1 - ahead)
    outer = (chip == 0) | (chip == chips - 1)

    inputs = [
        pltpu.make_async_copy(src, dst, in_sem.at[k])
        for k, (src, dst) in enumerate((
            (ld_hbm, ld_ref), (seg_hbm, seg_ref), (x_hbm, x_ref), (d_hbm, d_ref), (skip_hbm, skip_ref),
            (b_hbm, bc.at[0, 0]), (c_hbm, bc.at[1, 0])))
    ]
    for copy in inputs:
        copy.start()

    barrier = pltpu.get_barrier_semaphore()
    pl.semaphore_signal(barrier, inc=1, device_id={"head": mate}, device_id_type=MESH)
    close = peers == 8
    greeted = (1, 2, 4) if close else range(1, peers)
    for off in greeted:
        pl.semaphore_signal(barrier, inc=1, device_id={"ctx": me ^ off}, device_id_type=MESH)

    low = lax.broadcasted_iota(jnp.int32, (1, 128), 1) < head
    rows = lax.broadcasted_iota(jnp.int32, (tokens, tokens), 0)
    cols = lax.broadcasted_iota(jnp.int32, (tokens, tokens), 1)
    ones = jnp.where(rows <= cols, 1.0, 0.0).astype(BF)
    inputs[0].wait()
    ld = ld_ref[...]
    l0 = ld.astype(BF)
    r1 = ld - l0.astype(F32)
    l1 = r1.astype(BF)
    l2 = (r1 - l1.astype(F32)).astype(BF)
    acum = mm(l0, ones) + mm(l1, ones) + mm(l2, ones)
    acum_s[...] = acum
    acum_t = jnp.concatenate([acum, jnp.zeros((128 - heads, tokens), F32)], axis=0).T
    for p in range(pairs):
        acx[:, p * 128 : (p + 1) * 128] = jnp.where(
            low, acum_t[:, 2 * p : 2 * p + 1], acum_t[:, 2 * p + 1 : 2 * p + 2]
        )
    inputs[1].wait()
    seg_row = seg_ref[...].astype(F32)
    seg_col = jnp.broadcast_to(seg_row, (128, tokens)).T
    last = jnp.broadcast_to(seg_row[:, tokens - 1 : tokens], (1, hw))
    info[me, 0:1, :] = acx[tokens - 1 : tokens, 0:hw]
    info[me, 1:2, :] = acx[tokens - 1 : tokens, hw:width]
    info[me, 2:3, :] = last
    info[me, 3:4, :] = jnp.broadcast_to(seg_row[:, 0:1], (1, hw))

    inputs[2].wait()
    inputs[3].wait()
    end_mask = jnp.where(seg_col == last[:, 0:128], 1.0, 0.0)
    start_mask = jnp.where(seg_col == seg_row[:, 0:1], 1.0, 0.0)
    for p in range(pairs):
        s = slice(p * 128, (p + 1) * 128)
        a = acx[:, s]
        we = jnp.exp(a[tokens - 1 : tokens, :] - a) * end_mask
        we_s[:, s] = we
        w2[1, 0:tokens, s], w2[1, tokens : 2 * tokens, s] = split(x_ref[:, s].astype(F32) * we)
        ws = jnp.exp(a) * start_mask
        ws_s[:, s] = ws
        w2[0, 0:tokens, s], w2[0, tokens : 2 * tokens, s] = split(d_ref[:, s].astype(F32) * ws)

    def states(h, way):
        m_t = bc[way, h].T
        m_t = jnp.concatenate([m_t, m_t], axis=1)
        for u in range(h * PARTS, (h + 1) * PARTS):
            q = u % PARTS
            for k in range(2):
                s = slice(k * hw + q * cw, k * hw + (q + 1) * cw)
                fg[u, way, k] = mm(m_t, w2[1 - way, :, s])
            share(u, way)

    inputs[5].wait()
    inputs[6].wait()
    pl.semaphore_wait(barrier, len(greeted) + 1)

    bc_copies = []

    def swap_maps():
        for k in range(2):
            copy = pltpu.make_async_remote_copy(
                src_ref=bc.at[ways[k], 0], dst_ref=bc.at[ways[k], 1], send_sem=bc_send.at[k], recv_sem=bc_recv.at[k],
                device_id={"head": mate}, device_id_type=MESH)
            copy.start()
            bc_copies.append(copy)

    i_copies = []
    d_copies = {}

    def tell(off):
        copy = pltpu.make_async_remote_copy(
            src_ref=info.at[me], dst_ref=info.at[me], send_sem=i_send.at[off - 1], recv_sem=i_recv.at[off - 1],
            device_id={"ctx": me ^ off}, device_id_type=MESH)
        copy.start()
        i_copies.append(copy)

    def hear(off):
        src = me ^ off
        pltpu.make_async_remote_copy(
            src_ref=info.at[src], dst_ref=info.at[src], send_sem=i_send.at[off - 1], recv_sem=i_recv.at[off - 1],
            device_id={"ctx": src}, device_id_type=MESH).wait_recv()

    def give(src, dst, at):
        copy = pltpu.make_async_remote_copy(
            src_ref=src, dst_ref=dst, send_sem=d_send.at[at], recv_sem=d_recv.at[at],
            device_id={"ctx": sib}, device_id_type=MESH)
        copy.start()
        d_copies[at] = copy

    def share(u, way):
        at = 3 * u + (0 if way is ways[0] else 1)
        give(fg.at[u, way, 1 - core], got.at[u, jnp.where(way == core, 1 - core, 2)], at)

    def share_rest(u):
        give(fg.at[u, core, core], got.at[u, core], 3 * u + 2)

    swap_maps()
    tell(1)
    if close:
        pl.semaphore_signal(near_sem, inc=1, device_id={"ctx": me ^ 2}, device_id_type=MESH)
    for way in ways:
        states(0, way)
    if close:
        tell(2)
        tell(4)
        pl.semaphore_wait(near_sem, 1)
        tell(6)
    else:
        for off in range(2, peers):
            tell(off)
    for u in range(PARTS):
        share_rest(u)

    bias[...] = jnp.where(
        (rows >= cols) & (jnp.concatenate([seg_col] * (tokens // 128), axis=1) == seg_row), 0.0, -1e30
    )
    dsc[...] = jnp.zeros_like(dsc)
    inputs[4].wait()

    def seg_last(i):
        return info[i, 2:3, :]

    def seg_first(i):
        return info[i, 3:4, :]

    def table_step(p, carried):
        s = pl.ds(pl.multiple_of(p * 128, 128), 128)
        x = x_ref[:, s]
        d = d_ref[:, s]
        zero = jnp.zeros_like(x)
        total = dsc[...]
        for k in range(2):
            mine = low if k == 0 else jnp.logical_not(low)
            dm = jnp.where(mine, d, zero)
            a_col = acx[:, s][:, k * head : k * head + 1]
            a_row = acum_s[pl.ds(2 * p + k, 1), :]
            table = jnp.exp((a_col - a_row) + bias[...])
            tab[2 * p + k] = table
            total = total + mm(dm, x, NT) * table
        dsc[...] = total
        return carried

    def mix_step(p, carried):
        s = pl.ds(pl.multiple_of(p * 128, 128), 128)
        x = x_ref[:, s]
        d = d_ref[:, s]
        gain = jnp.where(low, skip_ref[2 * p], skip_ref[2 * p + 1])
        out = gain * x.astype(F32)
        gx = gain * d.astype(F32)
        zero = jnp.zeros_like(x)
        for k in range(2):
            mine = low if k == 0 else jnp.logical_not(low)
            mixed = (tab[2 * p + k] * score_s[...]).astype(BF)
            out = out + mm(mixed, jnp.where(mine, x, zero))
            gx = gx + mm(mixed, jnp.where(mine, d, zero), TN)
        ssd_acc[:, s] = out
        gx_acc[:, s] = gx
        return carried

    lax.fori_loop(0, EARLY, table_step, 0)

    hear(1)
    joined = jnp.where(seg_first(2 * chip + 1) == seg_last(2 * chip), 1.0, 0.0)

    def carry(i, k):
        return jnp.exp(info[i, pl.ds(k, 1), :]) * jnp.where(seg_first(i) == seg_last(i), joined, 0.0)

    sib_carry = carry(sib, core)
    my_carry = carry(me, core)
    t_copies = {}

    def code(u, way):
        c = slice((u % PARTS) * cw, (u % PARTS + 1) * cw)
        d_copies[3 * u + (0 if way is ways[0] else 1)].wait_recv()
        mine = jnp.full((1, cw), way, jnp.int32) == core
        kept = jnp.where(mine, sib_carry[:, c], 1.0)
        added = jnp.where(mine, 1.0, my_carry[:, c])
        encode(tbuf.at[u, way], kept * fg[u, way, core] + added * got[u, jnp.where(way == core, 2, core)])

    def message(u, off):
        other = chip ^ off
        at = u * (chips - 1) + off - 1
        t_copies[at] = pltpu.make_async_remote_copy(
            src_ref=tbuf.at[u, jnp.where(other > chip, 0, 1)], dst_ref=slots.at[at],
            send_sem=t_send.at[at], recv_sem=t_recv.at[at],
            device_id={"ctx": other * 2 + core}, device_id_type=MESH)
        return t_copies[at]

    def send(u, offs):
        for off in offs:
            message(u, off).start()

    direct = (1, 2) if close else range(1, chips)
    across = (3,) if close else ()

    for u in range(PARTS):
        for way in ways:
            code(u, way)
        send(u, direct)
    lax.fori_loop(EARLY, MIDDLE, table_step, 0)
    late_units = range(PARTS, units)
    bc_copies[0].wait_recv()
    states(1, ways[0])
    lax.fori_loop(MIDDLE, pairs, table_step, 0)
    for u in late_units:
        code(u, ways[0])
        if close:
            send(u, across)
            send(u, (2,))
            pl.when(outer)(message(u, 1).start)
    bc_copies[1].wait_recv()
    states(1, ways[1])

    b_full = jnp.concatenate([bc[0, 0], bc[0, 1]], axis=1)
    c_full = jnp.concatenate([bc[1, 0], bc[1, 1]], axis=1)
    score_s[...] = mm(c_full, b_full, NT)
    ds_hi, ds_lo = split(dsc[...])
    gb = mm(ds_hi, c_full, TN) + mm(ds_lo, c_full, TN)
    gc = mm(ds_hi, b_full) + mm(ds_lo, b_full)
    for h in range(2):
        gacc[0, h] = gb[:, h * n : (h + 1) * n]
        gacc[1, h] = gc[:, h * n : (h + 1) * n]

    for u in late_units:
        code(u, ways[1])
        if close:
            pl.when(jnp.logical_not(outer))(message(u, 1).start)
        else:
            send(u, direct)
    for u in range(PARTS):
        send(u, across)
    for u in late_units:
        share_rest(u)

    if close:
        for off in (2, 4, 6):
            hear(off)
            copy = pltpu.make_async_remote_copy(
                src_ref=info.at[me ^ off], dst_ref=info.at[me ^ off],
                send_sem=i_send.at[off], recv_sem=i_recv.at[off],
                device_id={"ctx": sib}, device_id_type=MESH)
            copy.start()
            i_copies.append(copy)

    s_copies = {}

    def pass_on(u, offs):
        for off in offs:
            at = u * (chips - 1) + off - 1
            t_copies[at].wait_recv()
            copy = pltpu.make_async_remote_copy(
                src_ref=slots.at[at], dst_ref=twin.at[at], send_sem=s_send.at[at], recv_sem=s_recv.at[at],
                device_id={"ctx": sib}, device_id_type=MESH)
            copy.start()
            s_copies[at] = copy

    lax.fori_loop(0, MIXED, mix_step, 0)
    for u in range(PARTS):
        pass_on(u, direct)
    lax.fori_loop(MIXED, pairs, mix_step, 0)

    for off in (3, 5, 7) if close else range(2, peers):
        hear(off)
    weights = []
    for off in range(1, chips):
        src = chip ^ off
        first = jnp.minimum(src, chip)
        final = jnp.maximum(src, chip)
        total = [jnp.zeros((1, hw), F32)] * 2
        for i in range(peers):
            within = (i >= 2 * first + 2) & (i < 2 * final)
            for k in range(2):
                total[k] = total[k] + jnp.where(within, info[i, pl.ds(core ^ k, 1), :], 0.0)
        linked = jnp.where(seg_last(2 * first + 1) == seg_first(2 * final), 1.0, 0.0)
        weights.append([jnp.exp(total[k]) * linked for k in range(2)])
    sib_both = [carry(sib, k) for k in range(2)]

    def gather(u, offs):
        c = slice((u % PARTS) * cw, (u % PARTS + 1) * cw)
        for k, ref in ((0, slots), (1, twin)):
            for off in offs:
                later = jnp.where((chip ^ off) < chip, 0, 1)
                at = u * (chips - 1) + off - 1
                if k:
                    s_copies[at].wait_recv()
                st[u, core ^ k, later] = st[u, core ^ k, later] + decode(ref.at[at], weights[off - 1][k][:, c])

    g_copies = []

    def send_off(which):
        encode(zbuf.at[which], gacc[which, 1])
        g_copy = pltpu.make_async_remote_copy(
            src_ref=zbuf.at[which], dst_ref=zrecv.at[which],
            send_sem=g_send.at[which], recv_sem=g_recv.at[which],
            device_id={"head": mate}, device_id_type=MESH)
        g_copy.start()
        g_copies.append(g_copy)

    def absorb(u, way):
        h, q = u // PARTS, u % PARTS
        c = slice(q * cw, (q + 1) * cw)
        moved = jnp.full((1, cw), way, jnp.int32) != core
        lhs = []
        rhs = []
        for k in range(2):
            s = slice(k * hw + q * cw, k * hw + (q + 1) * cw)
            keep = jnp.where(moved, sib_both[k][:, c], 1.0)
            add = jnp.where(moved, joined[:, c], 0.0)
            hi, lo = split(keep * st[u, k, way] + add * got[u, k])
            pieces[q, way, k, h * n : (h + 1) * n, :] = hi
            pieces[q, way, k, (2 + h) * n : (3 + h) * n, :] = lo
            w_hi = w2[way, 0:tokens, s]
            lhs += [w_hi, w2[way, tokens : 2 * tokens, s], w_hi]
            rhs += [hi, hi, lo]
        gacc[1 - way, h] = gacc[1 - way, h] + mm(jnp.concatenate(lhs, axis=1), jnp.concatenate(rhs, axis=1), NT)

    b_two = jnp.concatenate([b_full, b_full], axis=1)
    c_two = jnp.concatenate([c_full, c_full], axis=1)

    def outputs(q):
        for k in range(2):
            s = slice(k * hw + q * cw, k * hw + (q + 1) * cw)
            ssd_ref[:, s] = (ssd_acc[:, s] + ws_s[:, s] * mm(c_two, pieces[q, 0, k])).astype(BF)
            gx_ref[:, s] = (gx_acc[:, s] + we_s[:, s] * mm(b_two, pieces[q, 1, k])).astype(BF)

    st[...] = jnp.zeros_like(st)
    for u in range(PARTS):
        d_copies[3 * u + 2].wait_recv()
        gather(u, direct)
        absorb(u, ways[0])
    for u in late_units:
        pass_on(u, across)
        pass_on(u, direct)
    for u in late_units:
        d_copies[3 * u + 2].wait_recv()
        gather(u, direct)
        absorb(u, ways[0])
    send_off(1 - ways[0])
    for u in late_units:
        gather(u, across)
        absorb(u, ways[1])
    send_off(1 - ways[1])
    for u in range(PARTS):
        pass_on(u, across)
    for u in range(PARTS):
        gather(u, across)
        absorb(u, ways[1])
    for q in range(PARTS):
        outputs(q)

    one = jnp.ones((1, n), F32)
    for copy in g_copies:
        copy.wait_recv()
    for which, ref in ((0, gb_ref), (1, gc_ref)):
        ref[...] = (gacc[which, 0] + decode(zrecv.at[which], one)).astype(BF)

    for copy in bc_copies + i_copies + list(d_copies.values()) + list(t_copies.values()) + list(s_copies.values()) + g_copies:
        copy.wait_send()


def per_device(peers, inputs, log_decay, in_b, in_c, seg_ids, skip_gain, grad_out):
    tokens, width = inputs.shape
    heads = log_decay.shape[0]
    n = in_b.shape[1]
    hw = width // 2
    chips = peers // 2
    cw = hw // PARTS
    units = 2 * PARTS
    coded = n * cw // 128 + PAD
    vm = pl.BlockSpec(memory_space=pltpu.VMEM)
    dma = pltpu.SemaphoreType.DMA
    results = pl.pallas_call(
        functools.partial(kernel, peers),
        out_shape=(
            jax.ShapeDtypeStruct((tokens, width), BF),
            jax.ShapeDtypeStruct((tokens, width), BF),
            jax.ShapeDtypeStruct((tokens, n), BF),
            jax.ShapeDtypeStruct((tokens, n), BF),
        ),
        in_specs=[pl.BlockSpec(memory_space=pltpu.HBM)] * 7,
        out_specs=(vm, vm, vm, vm),
        scratch_shapes=[
            pltpu.VMEM((tokens, width), BF),
            pltpu.VMEM((heads, tokens), F32),
            pltpu.VMEM((1, tokens), jnp.int32),
            pltpu.SMEM((heads,), F32),
            pltpu.VMEM((tokens, width), BF),
            dma((7,)),
            pltpu.VMEM((2, 2, tokens, n), BF),
            pltpu.VMEM((peers, 4, hw), F32),
            pltpu.VMEM((heads, tokens), F32),
            pltpu.VMEM((tokens, width), F32),
            pltpu.VMEM((tokens, width), F32),
            pltpu.VMEM((tokens, width), F32),
            pltpu.VMEM((2, 2 * tokens, width), BF),
            pltpu.VMEM((tokens, tokens), F32),
            pltpu.VMEM((tokens, tokens), F32),
            pltpu.VMEM((tokens, tokens), F32),
            pltpu.VMEM((heads, tokens, tokens), F32),
            pltpu.VMEM((tokens, width), F32),
            pltpu.VMEM((tokens, width), F32),
            pltpu.VMEM((units, 2, 2, n, cw), F32),
            pltpu.VMEM((units, 3, n, cw), F32),
            pltpu.VMEM((units, 2, coded, 128), jnp.int16),
            pltpu.VMEM((units * (chips - 1), coded, 128), jnp.int16),
            pltpu.VMEM((units * (chips - 1), coded, 128), jnp.int16),
            pltpu.VMEM((units, 2, 2, n, cw), F32),
            pltpu.VMEM((PARTS, 2, 2, 4 * n, cw), BF),
            pltpu.VMEM((2, 2, tokens, n), F32),
            pltpu.VMEM((2, tokens * n // 128 + PAD, 128), jnp.int16),
            pltpu.VMEM((2, tokens * n // 128 + PAD, 128), jnp.int16),
            dma((2,)),
            dma((2,)),
            dma((peers - 1,)),
            dma((peers - 1,)),
            dma((3 * units,)),
            dma((3 * units,)),
            dma((units * (chips - 1),)),
            dma((units * (chips - 1),)),
            dma((units * (chips - 1),)),
            dma((units * (chips - 1),)),
            dma((2,)),
            dma((2,)),
            pltpu.SemaphoreType.REGULAR,
        ],
        compiler_params=pltpu.CompilerParams(
            collective_id=0, has_side_effects=True, vmem_limit_bytes=48 << 20
        ),
    )(*[pltpu.with_memory_space_constraint(a, pltpu.HBM) for a in (inputs, log_decay, in_b, in_c, seg_ids.reshape(1, tokens), skip_gain, grad_out)])
    hbm = pl.BlockSpec(memory_space=pltpu.HBM)
    return pl.pallas_call(
        hand_over,
        out_shape=tuple(jax.ShapeDtypeStruct(r.shape, r.dtype) for r in results),
        in_specs=[hbm] * 4,
        out_specs=(hbm,) * 4,
        scratch_shapes=[dma((4,))],
        compiler_params=pltpu.CompilerParams(vmem_limit_bytes=VMEM2),
    )(*results)


def hand_over(a, b, c, d, out_a, out_b, out_c, out_d, sem):
    copies = [
        pltpu.make_async_copy(src, dst, sem.at[k])
        for k, (src, dst) in enumerate(((a, out_a), (b, out_b), (c, out_c), (d, out_d)))
    ]
    for copy in copies:
        copy.start()
    for copy in copies:
        copy.wait()


def solution(mesh):
    return jax.shard_map(
        functools.partial(per_device, mesh.shape["ctx"]),
        mesh=mesh,
        in_specs=(
            P("ctx", "head"),
            P("head", "ctx"),
            P("ctx", "head"),
            P("ctx", "head"),
            P("ctx"),
            P("head"),
            P("ctx", "head"),
        ),
        out_specs=(P("ctx", "head"), P("ctx", "head"), P("ctx", "head"), P("ctx", "head")),
        check_vma=False,
    )
```
